32 devices in a mesh: grp: 2 (over core), seg: 16 (over z, y, x).
Axes of the slice: x: 2, y: 2, z: 4, core: 2. Of those that a mesh axis runs over, the one named last changes fastest.
Arguments:
- nodes: float32 [32, 256], P(('grp', 'seg')), may hold values from -6 to 6
- jac_inverse: float32 [128, 256, 256], P(('grp', 'seg')), may hold values from -3 to 3, as said below
- loss_rates: float32 [256], replicated, may hold values from 0.25 to 4
- rate_table: float32 [128, 256], P('grp'), may hold values from -6 to 6
- rate_index: int32 [128, 256], P(('grp', 'seg')), may hold values from 0 to 127
Outputs:
- new_nodes: float32 [32, 256], P(('grp', 'seg'))
- defects: float32 [32, 256], P(('grp', 'seg'))
The draws below stay inside these ranges and needn't reach their ends.
Inputs may be any that keep to these rules, and one draw needn't show every extreme that they name: `jac_inverse`: one 256 x 256 matrix a step.
All inputs are finite; a program needn't handle non-finite values.
Results may differ from the reference program's by a relative error of at most 0.0003.
Values sent between devices are 32-bit elements; how exact they have to be, the bound alone decides.
No kernel may reach another device: no remote copies, remote signals or barrier semaphores. Data moves between devices by JAX's collectives and lax.ppermute only.
A program may use at most 192 MiB of HBM per device.

```python
import math
import jax
import jax.numpy as jnp
from jax import lax

NB = 256
STEP_DEV = 4
SEGS = 32
TOTAL_STEPS = 128
NR = 128


def draw_jac_inverse(key, part):
    first, second, third = jax.random.split(jax.random.fold_in(key, 17), 3)
    diagonal = jax.random.uniform(first, (TOTAL_STEPS, NB), jnp.float32, 0.75, 1.5)
    common_weight = 0.5
    own_weight = 0.5
    eye = jnp.eye(NB, dtype=jnp.float32)
    common = jax.random.normal(second, (NB, NB), jnp.float32) * (common_weight / NB ** 0.5)
    own = jax.random.normal(third, (TOTAL_STEPS, NB, NB), jnp.float32) * (own_weight / NB ** 0.5)
    return (own + common[None]) * (1.0 - eye)[None] + diagonal[:, :, None] * eye[None]


def touch_ends(result, rng, least, high):
    index_at = [jax.random.randint(jax.random.fold_in(rng, axis), (), 0, length) for axis, length in enumerate(result.shape)]
    widest = result.shape.index(max(result.shape))
    beside = index_at[:widest] + [(index_at[widest] + 1) % result.shape[widest]] + index_at[widest + 1:]
    return result.at[tuple(index_at)].set(least).at[tuple(beside)].set(high)


def steps_of(stream_key, shape, pieces, smallest, largest):
    loudness = 1.0
    for position, parts in pieces:
        draws = jax.random.uniform(jax.random.fold_in(jax.random.fold_in(stream_key, 6), position), (parts,), jnp.float32, smallest / len(pieces), largest / len(pieces))
        loudness = loudness * jnp.repeat(jnp.exp(draws), shape[position] // parts).reshape((-1,) + (1,) * (len(shape) - 1 - position))
    return loudness


def gaussian(own_key, shape, spread, bound, cuts=(), kind=jnp.bfloat16):
    level = steps_of(own_key, shape, cuts, -0.22, 0.18) if cuts else 1.0
    array = jax.random.normal(own_key, shape, jnp.float32) * spread * level
    return jnp.minimum(jnp.maximum(array, -bound), bound).astype(kind)


def setup_inputs(seed: int = 0) -> dict:
    streams_of = jax.random.split(jax.random.key(seed), 6)
    nodes = gaussian(streams_of[0], (SEGS, NB), 1.0, 6.0, ((0, 32),), jnp.float32)
    jac_inverse = draw_jac_inverse(jax.random.fold_in(streams_of[5], 71), 0)
    loss_rates = jnp.clip(jnp.exp(jax.random.uniform(streams_of[2], (NB,), jnp.float32, math.log(0.25), math.log(4.0))), 0.25, 4.0)
    rate_table = gaussian(streams_of[3], (NR, NB), 1.0, 6.0, ((0, 2),), jnp.float32)
    rate_index = touch_ends(jax.random.randint(streams_of[4], (TOTAL_STEPS, NB), 0, NR), jax.random.fold_in(streams_of[4], 1), 0, NR - 1).astype(jnp.int32)
    return {"nodes": nodes, "jac_inverse": jac_inverse, "loss_rates": loss_rates, "rate_table": rate_table, "rate_index": rate_index}


def reference(nodes, jac_inverse, loss_rates, rate_table, rate_index):
    inv_len = 1.0 / TOTAL_STEPS
    src_scale = 0.25 / STEP_DEV
    sources = jnp.take_along_axis(rate_table, rate_index, axis=0)
    inverses = jac_inverse.reshape(SEGS, STEP_DEV, NB, NB)
    seg_sources = sources.reshape(SEGS, STEP_DEV, NB)

    def one_step(state, inputs):
        value, tangent = state
        matrix, source = inputs
        slope = jnp.tanh(value)
        weight = loss_rates * (1.0 - slope * slope)
        tangent_next = tangent - inv_len * jnp.dot(matrix, weight * tangent, precision=lax.Precision.HIGHEST)
        value_next = value + jnp.dot(matrix, src_scale * source - inv_len * loss_rates * slope, precision=lax.Precision.HIGHEST)
        return (value_next, tangent_next), None

    def one_segment(entry, inputs):
        start, matrices, source = inputs
        (final, tangent), unused = lax.scan(one_step, (start, entry - start), (matrices, source))
        exit_state = final + tangent
        return exit_state, (exit_state, final)

    unused, (new_nodes, finals) = lax.scan(one_segment, nodes[0], (nodes, inverses, seg_sources))
    following = jnp.concatenate([nodes[1:], jnp.zeros((1, NB), jnp.float32)], axis=0)
    return new_nodes, finals - following
```

```python
import functools
import jax
import jax.numpy as jnp
from jax import lax
from jax.experimental import pallas as pl
from jax.experimental.pallas import tpu as pltpu
from jax.sharding import PartitionSpec as P

AXES = ("grp", "seg")
PAD = 8
QUAD = 4
VMEM = pl.BlockSpec(memory_space=pltpu.VMEM)
SMEM = pl.BlockSpec(memory_space=pltpu.SMEM)


def dot(a, b, dims=((1,), (0,))):
    return lax.dot_general(
        a,
        b,
        (dims, ((), ())),
        precision=lax.Precision.HIGHEST,
        preferred_element_type=jnp.float32,
    )


def call(body, shapes, *args, scalars=0, scratch=()):
    out = tuple(jax.ShapeDtypeStruct(s, jnp.float32) for s in shapes)
    return pl.pallas_call(
        body,
        out_shape=out,
        in_specs=[SMEM] * scalars + [VMEM] * (len(args) - scalars),
        out_specs=tuple(VMEM for _ in out),
        scratch_shapes=list(scratch),
    )(*args)


def compose(earlier, later):
    width = later.shape[1]
    both = dot(earlier, later[:width])
    return both, later[width:]


def put_composed(ref, earlier, later):
    width = later.shape[1]
    both = dot(earlier, later[:width])
    ref[:width] = both[:width]
    ref[width:] = both[width:] + later[width:]


def local_body(inv_len, src_scale, place, own, other, index, nodes, loss, jac, out, final):
    steps, width, _ = jac.shape
    rows = own.shape[0]
    base = place[1] * rows
    level = lax.broadcasted_iota(jnp.int32, (rows, width), 0)
    start = jnp.broadcast_to(nodes[...], (PAD, width))
    state = start
    rates = loss[...]
    row = lax.broadcasted_iota(jnp.int32, (width, width), 0)
    col = lax.broadcasted_iota(jnp.int32, (width, width), 1)
    sens = jnp.where(row == col, 1.0, 0.0)
    for step in range(steps):
        want = index[step : step + 1, :]
        near = jnp.where(want - base == level, own[...], 0.0)
        far = jnp.where(want - (rows - base) == level, other[...], 0.0)
        source = jnp.sum(near + far, axis=0, keepdims=True)
        slope = jnp.tanh(state)
        weight = inv_len * (rates * (1.0 - slope * slope))
        drive = src_scale * source - inv_len * rates * slope
        both = dot(
            jnp.concatenate([sens * weight[:1], drive], axis=0), jac[step], ((1,), (1,))
        )
        sens = sens - both[:width]
        state = state + both[width:]
    first = place[0] == 0
    sens = jnp.where(first, 0.0, sens)
    out[:width] = sens
    out[width:] = state - dot(start, sens)
    final[...] = state[:1]


def quad_body(place, own, by1, by2, by3, total, prefix, held):
    member = lax.rem(place[0], QUAD)
    for k, part in enumerate((own, by1, by2, by3)):
        held[jnp.bitwise_xor(member, k)] = part[...]
    total[...] = held[0]

    @pl.when(member == 0)
    def _():
        prefix[...] = held[0]

    for k in range(1, QUAD):
        put_composed(total, total[...], held[k])

        @pl.when(member == k)
        def _():
            prefix[...] = total[...]


def octet_body(place, near, far, own_prefix, total, prefix):
    upper = lax.rem(lax.div(place[0], QUAD), 2) == 1

    @pl.when(upper)
    def _():
        put_composed(total, far[...], near[...])
        put_composed(prefix, far[...], own_prefix[...])

    @pl.when(jnp.logical_not(upper))
    def _():
        put_composed(total, near[...], far[...])
        prefix[...] = own_prefix[...]


def apply_body(entry, mapping, out):
    width = entry.shape[1]
    wide = jnp.broadcast_to(entry[...], (PAD, width))
    out[...] = (dot(wide, mapping[:width]) + mapping[width:])[:1]


def on_device(nodes, jac_inverse, loss_rates, rate_table, rate_index):
    steps, width, _ = jac_inverse.shape
    seg_count = lax.axis_size("seg")
    segments = lax.axis_size("grp") * seg_count
    inv_len = 1.0 / (steps * segments)
    src_scale = 0.25 / steps
    grp = lax.axis_index("grp")
    position = grp * seg_count + lax.axis_index("seg")
    place = jnp.stack([position, grp]).astype(jnp.int32)

    def swapped(array, by):
        return lax.ppermute(array, AXES, [(i, i ^ by) for i in range(segments)])

    other = swapped(rate_table, seg_count)
    mapped, final = call(
        functools.partial(local_body, inv_len, src_scale),
        [(width + PAD, width), (1, width)],
        place, rate_table, other, rate_index, nodes, loss_rates[None], jac_inverse,
        scalars=1,
    )
    shape = (width + PAD, width)
    parts = [swapped(mapped, k) for k in range(1, QUAD)]
    following = lax.ppermute(nodes, AXES, [(i + 1, i) for i in range(segments - 1)])
    quad, in_quad = call(
        quad_body, [shape, shape], place, mapped, *parts,
        scalars=1, scratch=[pltpu.VMEM((QUAD, *shape), jnp.float32)],
    )
    beside = swapped(quad, QUAD)
    octet, in_octet = call(
        octet_body, [shape, shape], place, quad, beside, in_quad, scalars=1
    )
    size = 2 * QUAD
    entry = jnp.zeros((1, width), jnp.float32)
    for hop in range(segments // size - 1):
        (leaving,) = call(apply_body, [(1, width)], entry, octet)
        pairs = [(hop * size + i, (hop + 1) * size + i) for i in range(size)]
        entry = entry + lax.ppermute(leaving, AXES, pairs)
    (update,) = call(apply_body, [(1, width)], entry, in_octet)
    return (update, final - following)


def solution(mesh):
    return jax.shard_map(
        on_device,
        mesh=mesh,
        in_specs=(
            P(("grp", "seg"), None),
            P(("grp", "seg"), None, None),
            P(),
            P("grp", None),
            P(("grp", "seg"), None),
        ),
        out_specs=(P(("grp", "seg"), None), P(("grp", "seg"), None)),
        check_vma=False,
    )
```

```python
import functools
import jax
import jax.numpy as jnp
from jax import lax
from jax.experimental import pallas as pl
from jax.experimental.pallas import tpu as pltpu
from jax.sharding import PartitionSpec as P

AXES = ("grp", "seg")
PAD = 8
QUAD = 4
VMEM = pl.BlockSpec(memory_space=pltpu.VMEM)
HBM = pl.BlockSpec(memory_space=pltpu.HBM)
F32 = jnp.float32


def halves(a):
    high = a.astype(jnp.bfloat16)
    return high, (a - high.astype(jnp.float32)).astype(jnp.bfloat16)


def dot(a, b, dims=((1,), (0,))):
    def one(x, y):
        return lax.dot_general(
            x, y, (dims, ((), ())), preferred_element_type=jnp.float32
        )

    (ah, al), (bh, bl) = halves(a), halves(b)
    return one(ah, bh) + (one(ah, bl) + one(al, bh))


def times(row, mat):
    n = mat.shape[0]
    on = lax.broadcasted_iota(jnp.int32, (n, n), 0) == lax.broadcasted_iota(
        jnp.int32, (n, n), 1
    )
    column = jnp.sum(jnp.where(on, row, 0.0), axis=1, keepdims=True)
    return jnp.sum(mat * column, axis=0, keepdims=True)


def call(body, shapes, *args, scratch=(), raw=False):
    out = tuple(jax.ShapeDtypeStruct(*s) for s in shapes)
    return pl.pallas_call(
        body,
        out_shape=out,
        in_specs=[HBM if raw else VMEM] * len(args),
        out_specs=tuple(VMEM for _ in out),
        scratch_shapes=list(scratch),
        compiler_params=pltpu.CompilerParams(vmem_limit_bytes=8 << 20),
    )(*args)


def where_am_i():
    return lax.axis_index("grp") * lax.axis_size("seg") + lax.axis_index("seg")


def put_composed(ref, earlier, later):
    width = later.shape[1]
    both = dot(earlier, later[:width])
    ref[:width] = both[:width]
    ref[width:] = both[width:] + later[width:]


def lookup(table, index, base):
    rows, width = table.shape
    level = lax.broadcasted_iota(jnp.int32, (rows, width), 0) + base
    kept = table[...]
    found = [
        jnp.sum(jnp.where(index[k : k + 1, :] == level, kept, 0.0), axis=0, keepdims=True)
        for k in range(index.shape[0])
    ]
    return jnp.concatenate(found, axis=0)


def early_body(
    inv_len, nodes_in, loss_in, jac_in, own_in, index_in,
    nodes, loss, jac, index, near, sens, state, own, sems,
):
    steps, width, _ = jac.shape
    copies = [
        pltpu.make_async_copy(src, dst, sems.at[k])
        for k, (src, dst) in enumerate(
            [(nodes_in, nodes), (loss_in, loss), (jac_in.at[0], jac.at[0])]
            + [(own_in, own), (index_in, index)]
            + [(jac_in.at[pl.ds(1, steps - 1)], jac.at[pl.ds(1, steps - 1)])]
        )
    ]
    for copy in copies:
        copy.start()
    for copy in copies[:3]:
        copy.wait()
    start = jnp.broadcast_to(nodes[...], (PAD, width))
    rates = loss[...]
    slope = jnp.tanh(start)
    weight = inv_len * (rates * (1.0 - slope * slope))
    row = lax.broadcasted_iota(jnp.int32, (width, width), 0)
    col = lax.broadcasted_iota(jnp.int32, (width, width), 1)
    first = jnp.where(row == col, weight[:1], 0.0)
    both = dot(
        jnp.concatenate([first, -inv_len * rates * slope], axis=0), jac[0], ((1,), (1,))
    )
    sens[...] = jnp.where(row == col, 1.0, 0.0) - both[:width]
    state[...] = start + both[width:]
    for copy in copies[3:5]:
        copy.wait()
    near[...] = lookup(own, index, lax.axis_index("grp") * own.shape[0])
    copies[5].wait()


def local_body(
    inv_len, src_scale, other, nodes, loss, jac, index, near, sens_in, state_in,
    out, final, kept,
):
    steps, width, _ = jac.shape
    rows = other.shape[0]
    source = near[...] + lookup(other, index, (1 - lax.axis_index("grp")) * rows)
    rates = loss[...]
    sens = sens_in[...]
    spread = jnp.sum(jac[0] * (src_scale * source[:1]), axis=1, keepdims=True)
    on = lax.broadcasted_iota(jnp.int32, (width, width), 0) == lax.broadcasted_iota(
        jnp.int32, (width, width), 1
    )
    state = state_in[...] + jnp.sum(jnp.where(on, spread, 0.0), axis=0, keepdims=True)
    for step in range(1, steps):
        slope = jnp.tanh(state)
        weight = inv_len * (rates * (1.0 - slope * slope))
        drive = src_scale * source[step : step + 1] - inv_len * rates * slope
        both = dot(
            jnp.concatenate([sens * weight[:1], drive], axis=0), jac[step], ((1,), (1,))
        )
        sens = sens - both[:width]
        state = state + both[width:]
    sens = jnp.where(where_am_i() == 0, 0.0, sens)
    out[:width] = sens
    out[width:] = state - jnp.broadcast_to(times(nodes[...], sens), state.shape)
    final[...] = state[:1]
    kept[...] = nodes[...]


def quad_body(own, by1, by2, by3, final, following, total, prefix, defect, held):
    member = lax.rem(where_am_i(), QUAD)
    for k, part in enumerate((own, by1, by2, by3)):
        held[jnp.bitwise_xor(member, k)] = part[...]
    total[...] = held[0]
    defect[...] = final[...] - following[...]

    @pl.when(member == 0)
    def _():
        prefix[...] = held[0]

    for k in range(1, QUAD):
        put_composed(total, total[...], held[k])

        @pl.when(member == k)
        def _():
            prefix[...] = total[...]


def octet_body(near, far, own_prefix, total, prefix, leaving):
    upper = lax.rem(lax.div(where_am_i(), QUAD), 2) == 1
    width = near.shape[1]

    @pl.when(upper)
    def _():
        put_composed(total, far[...], near[...])
        put_composed(prefix, far[...], own_prefix[...])

    @pl.when(jnp.logical_not(upper))
    def _():
        put_composed(total, near[...], far[...])
        prefix[...] = own_prefix[...]

    leaving[...] = total[width : width + 1]


def apply_body(entry, mapping, out):
    width = entry.shape[1]
    out[...] = times(entry[...], mapping[:width]) + mapping[width : width + 1]


def add_apply_body(before, extra, mapping, entry, out):
    width = before.shape[1]
    entry[...] = before[...] + extra[...]
    out[...] = times(entry[...], mapping[:width]) + mapping[width : width + 1]


def on_device(nodes, jac_inverse, loss_rates, rate_table, rate_index):
    steps, width, _ = jac_inverse.shape
    seg_count = lax.axis_size("seg")
    segments = lax.axis_size("grp") * seg_count
    inv_len = 1.0 / (steps * segments)
    src_scale = 0.25 / steps

    def swapped(array, by):
        return lax.ppermute(array, AXES, [(i, i ^ by) for i in range(segments)])

    other = swapped(rate_table, seg_count)
    shape = ((width + PAD, width), F32)
    line = ((1, width), F32)
    early = call(
        functools.partial(early_body, inv_len),
        [
            line, line, (jac_inverse.shape, F32), (rate_index.shape, jnp.int32),
            ((steps, width), F32), ((width, width), F32), ((PAD, width), F32),
        ],
        *(
            pltpu.with_memory_space_constraint(array, pltpu.HBM)
            for array in (nodes, loss_rates[None], jac_inverse, rate_table, rate_index)
        ),
        scratch=[pltpu.VMEM(rate_table.shape, F32), pltpu.SemaphoreType.DMA((6,))],
        raw=True,
    )
    mapped, final, kept = call(
        functools.partial(local_body, inv_len, src_scale),
        [shape, line, line], other, *early,
    )
    parts = [swapped(mapped, k) for k in range(1, QUAD)]
    following = lax.ppermute(kept, AXES, [(i + 1, i) for i in range(segments - 1)])
    quad, in_quad, defect = call(
        quad_body, [shape, shape, line], mapped, *parts, final, following,
        scratch=[pltpu.VMEM((QUAD, *shape[0]), F32)],
    )
    beside = swapped(quad, QUAD)
    octet, in_octet, leaving = call(
        octet_body, [shape, shape, line], quad, beside, in_quad
    )
    size = 2 * QUAD
    hops = segments // size - 1
    entry = None
    for hop in range(hops):
        pairs = [(hop * size + i, (hop + 1) * size + i) for i in range(size)]
        landed = lax.ppermute(leaving, AXES, pairs)
        mapping = octet if hop < hops - 1 else in_octet
        if entry is None:
            entry = landed
            (leaving,) = call(apply_body, [line], entry, mapping)
        else:
            entry, leaving = call(add_apply_body, [line, line], entry, landed, mapping)
    return (leaving, defect)


def solution(mesh):
    return jax.shard_map(
        on_device,
        mesh=mesh,
        in_specs=(
            P(("grp", "seg"), None),
            P(("grp", "seg"), None, None),
            P(),
            P("grp", None),
            P(("grp", "seg"), None),
        ),
        out_specs=(P(("grp", "seg"), None), P(("grp", "seg"), None)),
        check_vma=False,
    )
```

```python
import functools
import jax
import jax.numpy as jnp
from jax import lax
from jax.experimental import pallas as pl
from jax.experimental.pallas import tpu as pltpu
from jax.sharding import PartitionSpec as P


AXES = ("grp", "seg")
PAD = 8
QUAD = 4
VMEM = pl.BlockSpec(memory_space=pltpu.VMEM)
HBM = pl.BlockSpec(memory_space=pltpu.HBM)
F32 = jnp.float32


def halves(a):
    high = a.astype(jnp.bfloat16)
    return high, (a - high.astype(jnp.float32)).astype(jnp.bfloat16)


def dot(a, b, dims=((1,), (0,))):
    def one(x, y):
        return lax.dot_general(
            x, y, (dims, ((), ())), preferred_element_type=jnp.float32
        )

    (ah, al), (bh, bl) = halves(a), halves(b)
    return one(ah, bh) + (one(ah, bl) + one(al, bh))


def times(row, mat):
    n = mat.shape[0]
    on = lax.broadcasted_iota(jnp.int32, (n, n), 0) == lax.broadcasted_iota(
        jnp.int32, (n, n), 1
    )
    column = jnp.sum(jnp.where(on, row, 0.0), axis=1, keepdims=True)
    return jnp.sum(mat * column, axis=0, keepdims=True)


def call(body, shapes, *args, scratch=(), raw=False):
    out = tuple(jax.ShapeDtypeStruct(*s) for s in shapes)
    return pl.pallas_call(
        body,
        out_shape=out,
        in_specs=[HBM if raw else VMEM] * len(args),
        out_specs=tuple(VMEM for _ in out),
        scratch_shapes=list(scratch),
        compiler_params=pltpu.CompilerParams(vmem_limit_bytes=8 << 20),
    )(*args)


def where_am_i():
    return lax.axis_index("grp") * lax.axis_size("seg") + lax.axis_index("seg")


def put_composed(ref, earlier, later):
    width = later.shape[1]
    both = dot(earlier, later[:width])
    ref[:width] = both[:width]
    ref[width:] = both[width:] + later[width:]


def lookup(table, index, base):
    rows, width = table.shape
    level = lax.broadcasted_iota(jnp.int32, (rows, width), 0) + base
    kept = table[...]
    found = [
        jnp.sum(jnp.where(index[k : k + 1, :] == level, kept, 0.0), axis=0, keepdims=True)
        for k in range(index.shape[0])
    ]
    return jnp.concatenate(found, axis=0)


def early_body(
    inv_len, nodes_in, loss_in, jac_in, own_in, index_in,
    nodes, loss, jac, index, near, sens, state, own, sems,
):
    steps, width, _ = jac.shape
    copies = [
        pltpu.make_async_copy(src, dst, sems.at[k])
        for k, (src, dst) in enumerate(
            [(nodes_in, nodes), (loss_in, loss), (jac_in.at[0], jac.at[0])]
            + [(own_in, own), (index_in, index)]
            + [(jac_in.at[pl.ds(1, steps - 1)], jac.at[pl.ds(1, steps - 1)])]
        )
    ]
    for copy in copies:
        copy.start()
    for copy in copies[:3]:
        copy.wait()
    start = jnp.broadcast_to(nodes[...], (PAD, width))
    rates = loss[...]
    slope = jnp.tanh(start)
    weight = inv_len * (rates * (1.0 - slope * slope))
    row = lax.broadcasted_iota(jnp.int32, (width, width), 0)
    col = lax.broadcasted_iota(jnp.int32, (width, width), 1)
    first = jnp.where(row == col, weight[:1], 0.0)
    both = dot(
        jnp.concatenate([first, -inv_len * rates * slope], axis=0), jac[0], ((1,), (1,))
    )
    sens[...] = jnp.where(row == col, 1.0, 0.0) - both[:width]
    state[...] = start + both[width:]
    for copy in copies[3:5]:
        copy.wait()
    near[...] = lookup(own, index, lax.axis_index("grp") * own.shape[0])
    copies[5].wait()


def local_body(
    inv_len, src_scale, other, nodes, loss, jac, index, near, sens_in, state_in,
    out, final, kept,
):
    steps, width, _ = jac.shape
    rows = other.shape[0]
    source = near[...] + lookup(other, index, (1 - lax.axis_index("grp")) * rows)
    rates = loss[...]
    sens = sens_in[...]
    spread = jnp.sum(jac[0] * (src_scale * source[:1]), axis=1, keepdims=True)
    on = lax.broadcasted_iota(jnp.int32, (width, width), 0) == lax.broadcasted_iota(
        jnp.int32, (width, width), 1
    )
    state = state_in[...] + jnp.sum(jnp.where(on, spread, 0.0), axis=0, keepdims=True)
    for step in range(1, steps):
        slope = jnp.tanh(state)
        weight = inv_len * (rates * (1.0 - slope * slope))
        drive = src_scale * source[step : step + 1] - inv_len * rates * slope
        both = dot(
            jnp.concatenate([sens * weight[:1], drive], axis=0), jac[step], ((1,), (1,))
        )
        sens = sens - both[:width]
        state = state + both[width:]
    sens = jnp.where(where_am_i() == 0, 0.0, sens)
    out[:width] = sens
    out[width:] = state - jnp.broadcast_to(times(nodes[...], sens), state.shape)
    out[width + 1 : width + 2] = nodes[...]
    final[...] = state[:1]
    kept[...] = nodes[...]


def in_order(held, parts):
    member = lax.rem(where_am_i(), QUAD)
    for k, part in enumerate(parts):
        held[jnp.bitwise_xor(member, k)] = part[...]


def follow(entry, mapping):
    width = mapping.shape[1]
    return times(entry, mapping[:width]) + mapping[width : width + 1]


def quad_body(own, by1, by2, by3, final, following, total, leaving, defect, held):
    width = own.shape[1]
    in_order(held, (own, by1, by2, by3))
    member = lax.rem(where_am_i(), QUAD)
    beside = held[lax.rem(member + 1, QUAD), width + 1 : width + 2]
    last = member == QUAD - 1
    defect[...] = final[...] - jnp.where(last, following[...], beside)
    first = where_am_i() < QUAD

    @pl.when(first)
    def _():
        state = held[0, width : width + 1]
        for k in range(1, QUAD):
            state = follow(state, held[k])
        leaving[...] = state
        total[...] = jnp.zeros_like(total)

    @pl.when(jnp.logical_not(first))
    def _():
        put_composed(total, held[0], held[1])
        put_composed(held.at[0], held[2], held[3])
        put_composed(total, total[...], held[0])
        leaving[...] = total[width : width + 1]


def is_upper():
    return lax.rem(lax.div(where_am_i(), QUAD), 2) == 1


def prefix_body(own, by1, by2, by3, far, after, prefix, held):
    in_order(held, (own, by1, by2, by3))
    member = lax.rem(where_am_i(), QUAD)
    prefix[...] = held[0]

    @pl.when(jnp.logical_and(is_upper(), where_am_i() >= 2 * QUAD))
    def _():
        put_composed(prefix, far[...], held[0])

    for k in range(1, QUAD):

        @pl.when(member >= k)
        def _():
            put_composed(prefix, prefix[...], held[k])


def follow_body(entry, mapping, out):
    out[...] = follow(entry[...], mapping[...])


def follow_two_body(entry, own, far, out):
    upper = is_upper()

    @pl.when(upper)
    def _():
        out[...] = follow(follow(entry[...], far[...]), own[...])

    @pl.when(jnp.logical_not(upper))
    def _():
        out[...] = follow(follow(entry[...], own[...]), far[...])


def last_body(targets, *refs):
    *arrived, mapping, out = refs
    octet = lax.div(where_am_i(), 2 * QUAD)
    entry = jnp.zeros_like(out)
    for target, row in zip(targets, arrived):
        here = octet == target
        if target == 0:
            here = jnp.logical_and(here, is_upper())
        entry = jnp.where(here, row[...], entry)
    out[...] = follow(entry, mapping[...])


def on_device(nodes, jac_inverse, loss_rates, rate_table, rate_index):
    steps, width, _ = jac_inverse.shape
    seg_count = lax.axis_size("seg")
    segments = lax.axis_size("grp") * seg_count
    inv_len = 1.0 / (steps * segments)
    src_scale = 0.25 / steps

    def swapped(array, by):
        return lax.ppermute(array, AXES, [(i, i ^ by) for i in range(segments)])

    other = swapped(rate_table, seg_count)
    shape = ((width + PAD, width), F32)
    line = ((1, width), F32)
    early = call(
        functools.partial(early_body, inv_len),
        [
            line, line, (jac_inverse.shape, F32), (rate_index.shape, jnp.int32),
            ((steps, width), F32), ((width, width), F32), ((PAD, width), F32),
        ],
        *(
            pltpu.with_memory_space_constraint(array, pltpu.HBM)
            for array in (nodes, loss_rates[None], jac_inverse, rate_table, rate_index)
        ),
        scratch=[pltpu.VMEM(rate_table.shape, F32), pltpu.SemaphoreType.DMA((6,))],
        raw=True,
    )
    mapped, final, kept = call(
        functools.partial(local_body, inv_len, src_scale),
        [shape, line, line], other, *early,
    )
    parts = [swapped(mapped, k) for k in range(1, QUAD)]
    ends = range(QUAD, segments, QUAD)
    following = lax.ppermute(kept, AXES, [(i, i - 1) for i in ends])
    held = pltpu.VMEM((QUAD, *shape[0]), F32)
    quad, leaving, defect = call(
        quad_body, [shape, line, line], mapped, *parts, final, following, scratch=[held]
    )
    size = 2 * QUAD
    octets = segments // size

    def moved(array, start, by, count):
        pairs = [(start + k, start + k + by) for k in range(count)]
        return lax.ppermute(array, AXES, pairs)

    row = swapped(leaving, QUAD)
    far = swapped(quad, QUAD)
    arrived = [(0, row)]
    (leaving,) = call(follow_body, [line], row, quad)
    row = moved(leaving, QUAD, size, QUAD) + moved(leaving, QUAD, QUAD, QUAD)
    arrived.append((1, row))
    for octet in range(1, octets - 1):
        (leaving,) = call(follow_two_body, [line], row, quad, far)
        if octet < octets - 2:
            row = swapped(leaving, (octet ^ (octet + 1)) * size)
        else:
            row = moved(leaving, octet * size, size, size)
        arrived.append((octet + 1, row))
    (prefix,) = call(prefix_body, [shape], mapped, *parts, far, leaving, scratch=[held])
    targets, rows = zip(*arrived)
    (update,) = call(functools.partial(last_body, targets), [line], *rows, prefix)
    return (update, defect)


def solution(mesh):
    return jax.shard_map(
        on_device,
        mesh=mesh,
        in_specs=(
            P(("grp", "seg"), None),
            P(("grp", "seg"), None, None),
            P(),
            P("grp", None),
            P(("grp", "seg"), None),
        ),
        out_specs=(P(("grp", "seg"), None), P(("grp", "seg"), None)),
        check_vma=False,
    )
```

```python
import functools
import jax
import jax.numpy as jnp
from jax import lax
from jax.experimental import pallas as pl
from jax.experimental.pallas import tpu as pltpu
from jax.sharding import PartitionSpec as P


AXES = ("grp", "seg")
PAD = 8
QUAD = 4
VMEM = pl.BlockSpec(memory_space=pltpu.VMEM)
HBM = pl.BlockSpec(memory_space=pltpu.HBM)
F32 = jnp.float32


def halves(a):
    high = a.astype(jnp.bfloat16)
    return high, (a - high.astype(jnp.float32)).astype(jnp.bfloat16)


def dot(a, b, dims=((1,), (0,))):
    def one(x, y):
        return lax.dot_general(
            x, y, (dims, ((), ())), preferred_element_type=jnp.float32
        )

    (ah, al), (bh, bl) = halves(a), halves(b)
    return one(ah, bh) + (one(ah, bl) + one(al, bh))


def times(row, mat):
    n = mat.shape[0]
    on = lax.broadcasted_iota(jnp.int32, (n, n), 0) == lax.broadcasted_iota(
        jnp.int32, (n, n), 1
    )
    column = jnp.sum(jnp.where(on, row, 0.0), axis=1, keepdims=True)
    return jnp.sum(mat * column, axis=0, keepdims=True)


def call(body, shapes, *args, scratch=(), raw=False):
    out = tuple(jax.ShapeDtypeStruct(*s) for s in shapes)
    return pl.pallas_call(
        body,
        out_shape=out,
        in_specs=[HBM if raw else VMEM] * len(args),
        out_specs=tuple(VMEM for _ in out),
        scratch_shapes=list(scratch),
        compiler_params=pltpu.CompilerParams(vmem_limit_bytes=8 << 20),
    )(*args)


def where_am_i():
    return lax.axis_index("grp") * lax.axis_size("seg") + lax.axis_index("seg")


def put_composed(ref, earlier, later):
    width = later.shape[1]
    both = dot(earlier, later[:width])
    ref[:width] = both[:width]
    ref[width:] = both[width:] + later[width:]


def lookup(table, index, base):
    rows, width = table.shape
    level = lax.broadcasted_iota(jnp.int32, (rows, width), 0) + base
    kept = table[...]
    found = [
        jnp.sum(jnp.where(index[k : k + 1, :] == level, kept, 0.0), axis=0, keepdims=True)
        for k in range(index.shape[0])
    ]
    return jnp.concatenate(found, axis=0)


def early_body(
    inv_len, nodes_in, loss_in, jac_in, own_in, index_in,
    nodes, loss, jac, index, near, sens, state, own, sems,
):
    steps, width, _ = jac.shape
    copies = [
        pltpu.make_async_copy(src, dst, sems.at[k])
        for k, (src, dst) in enumerate(
            [(nodes_in, nodes), (loss_in, loss), (jac_in.at[0], jac.at[0])]
            + [(own_in, own), (index_in, index)]
            + [(jac_in.at[pl.ds(1, steps - 1)], jac.at[pl.ds(1, steps - 1)])]
        )
    ]
    for copy in copies:
        copy.start()
    for copy in copies[:3]:
        copy.wait()
    start = jnp.broadcast_to(nodes[...], (PAD, width))
    rates = loss[...]
    slope = jnp.tanh(start)
    weight = inv_len * (rates * (1.0 - slope * slope))
    row = lax.broadcasted_iota(jnp.int32, (width, width), 0)
    col = lax.broadcasted_iota(jnp.int32, (width, width), 1)
    first = jnp.where(row == col, weight[:1], 0.0)
    both = dot(
        jnp.concatenate([first, -inv_len * rates * slope], axis=0), jac[0], ((1,), (1,))
    )
    sens[...] = jnp.where(row == col, 1.0, 0.0) - both[:width]
    state[...] = start + both[width:]
    for copy in copies[3:5]:
        copy.wait()
    near[...] = lookup(own, index, lax.axis_index("grp") * own.shape[0])
    copies[5].wait()


def local_body(
    inv_len, src_scale, other, nodes, loss, jac, index, near, sens_in, state_in,
    top, bottom, final,
):
    steps, width, _ = jac.shape
    cut = top.shape[0]
    rows = other.shape[0]
    source = near[...] + lookup(other, index, (1 - lax.axis_index("grp")) * rows)
    rates = loss[...]
    sens = sens_in[...]
    spread = jnp.sum(jac[0] * (src_scale * source[:1]), axis=1, keepdims=True)
    on = lax.broadcasted_iota(jnp.int32, (width, width), 0) == lax.broadcasted_iota(
        jnp.int32, (width, width), 1
    )
    state = state_in[...] + jnp.sum(jnp.where(on, spread, 0.0), axis=0, keepdims=True)
    for step in range(1, steps):
        slope = jnp.tanh(state)
        weight = inv_len * (rates * (1.0 - slope * slope))
        drive = src_scale * source[step : step + 1] - inv_len * rates * slope
        both = dot(
            jnp.concatenate([sens * weight[:1], drive], axis=0), jac[step], ((1,), (1,))
        )
        sens = sens - both[:width]
        state = state + both[width:]
    sens = jnp.where(where_am_i() == 0, 0.0, sens)
    top[...] = sens[:cut]
    bottom[: width - cut] = sens[cut:]
    offset = state - jnp.broadcast_to(times(nodes[...], sens), state.shape)
    bottom[width - cut :] = offset
    bottom[width - cut + 1 : width - cut + 2] = nodes[...]
    final[...] = state[:1]


def in_order(held, parts):
    member = lax.rem(where_am_i(), QUAD)
    cut = parts[0].shape[0]
    for k in range(QUAD):
        place = jnp.bitwise_xor(member, k)
        held[place, :cut] = parts[2 * k][...]
        held[place, cut:] = parts[2 * k + 1][...]


def follow(entry, mapping):
    width = mapping.shape[1]
    return times(entry, mapping[:width]) + mapping[width : width + 1]


def first_exit_body(*refs):
    *parts, leaving = refs
    place = where_am_i()
    width = leaving.shape[1]
    cut = parts[0].shape[0]

    def step(state, k):
        upper, lower = parts[2 * k : 2 * k + 2]
        rest = width - cut
        n = lax.broadcasted_iota(jnp.int32, (width, width), 0)
        on = n == lax.broadcasted_iota(jnp.int32, (width, width), 1)
        column = jnp.sum(jnp.where(on, state, 0.0), axis=1, keepdims=True)
        return (
            jnp.sum(upper[...] * column[:cut], axis=0, keepdims=True)
            + jnp.sum(lower[:rest] * column[cut:], axis=0, keepdims=True)
            + lower[rest : rest + 1]
        )

    for member in range(QUAD):

        @pl.when(place == member)
        def _():
            state = parts[2 * member + 1][width - cut : width - cut + 1]
            for k in range(1, QUAD):
                state = step(state, member ^ k)
            leaving[...] = state


def quad_body(*refs):
    *parts, after, total, beside, held = refs
    width = total.shape[1]
    in_order(held, parts)
    member = lax.rem(where_am_i(), QUAD)
    node = width + 1
    beside[...] = held[lax.rem(member + 1, QUAD), node : node + 1]

    @pl.when(where_am_i() < QUAD)
    def _():
        total[...] = jnp.zeros_like(total)

    @pl.when(where_am_i() >= QUAD)
    def _():
        head = held[0, node : node + 1]
        put_composed(total, held[0], held[1])
        put_composed(held.at[0], held[2], held[3])
        put_composed(total, total[...], held[0])
        total[node : node + 1] = head


def is_upper():
    return lax.rem(lax.div(where_am_i(), QUAD), 2) == 1


def prefix_body(*refs):
    *parts, far, after, prefix, held = refs
    in_order(held, parts)
    member = lax.rem(where_am_i(), QUAD)
    prefix[...] = held[0]

    @pl.when(jnp.logical_and(is_upper(), where_am_i() >= 2 * QUAD))
    def _():
        put_composed(prefix, far[...], held[0])

    for k in range(1, QUAD):

        @pl.when(member >= k)
        def _():
            put_composed(prefix, prefix[...], held[k])


def follow_body(entry, mapping, out):
    out[...] = follow(entry[...], mapping[...])


def octet_exit_body(entry, own, far, out):
    upper = is_upper()
    width = own.shape[1]
    at = entry[:1]

    @pl.when(upper)
    def _():
        out[:1] = follow(follow(at, far[...]), own[...])
        out[1:2] = far[width + 1 : width + 2]

    @pl.when(jnp.logical_not(upper))
    def _():
        out[:1] = follow(follow(at, own[...]), far[...])
        out[1:2] = own[width + 1 : width + 2]

    out[2:] = jnp.zeros_like(out[2:])


def last_body(targets, sources, *refs):
    *arrived, final, beside, far, back, mapping, out, defect = refs
    place = where_am_i()
    width = out.shape[1]
    member = lax.rem(place, QUAD)
    octet = lax.div(place, 2 * QUAD)
    entry = jnp.zeros_like(out)
    following = jnp.where(member == QUAD - 1, far[width + 1 : width + 2], beside[...])
    following = jnp.where(is_upper() & (member == QUAD - 1), back[...], following)
    for target, row in zip(targets, arrived):
        here = octet == target
        if target == 0:
            here = jnp.logical_and(here, is_upper())
        entry = jnp.where(here, row[:1], entry)
    for source, k in sources:
        ends = place == 2 * QUAD * (source + 1) - 1
        following = jnp.where(ends, arrived[k][1:2], following)
    out[...] = follow(entry, mapping[...])
    defect[...] = final[...] - following


def on_device(nodes, jac_inverse, loss_rates, rate_table, rate_index):
    steps, width, _ = jac_inverse.shape
    seg_count = lax.axis_size("seg")
    segments = lax.axis_size("grp") * seg_count
    inv_len = 1.0 / (steps * segments)
    src_scale = 0.25 / steps

    def swapped(array, by):
        return lax.ppermute(array, AXES, [(i, i ^ by) for i in range(segments)])

    other = swapped(rate_table, seg_count)
    shape = ((width + PAD, width), F32)
    line = ((1, width), F32)
    early = call(
        functools.partial(early_body, inv_len),
        [
            line, line, (jac_inverse.shape, F32), (rate_index.shape, jnp.int32),
            ((steps, width), F32), ((width, width), F32), ((PAD, width), F32),
        ],
        *(
            pltpu.with_memory_space_constraint(array, pltpu.HBM)
            for array in (nodes, loss_rates[None], jac_inverse, rate_table, rate_index)
        ),
        scratch=[pltpu.VMEM(rate_table.shape, F32), pltpu.SemaphoreType.DMA((6,))],
        raw=True,
    )
    cut = width // 2
    halves = [((cut, width), F32), ((width - cut + PAD, width), F32)]
    top, bottom, final = call(
        functools.partial(local_body, inv_len, src_scale),
        [*halves, line], other, *early,
    )
    top1 = swapped(top, 1)
    bottom2 = swapped(bottom, 2)
    bottom1 = swapped(bottom, 1)
    top2 = swapped(top, 2)
    top3 = swapped(top1, 2)
    bottom3 = swapped(bottom2, 1)
    parts = [top, bottom, top1, bottom1, top2, bottom2, top3, bottom3]
    (leaving,) = call(first_exit_body, [line], *parts)
    size = 2 * QUAD
    octets = segments // size

    def moved(array, start, by, count):
        pairs = [(start + k, start + k + by) for k in range(count)]
        return lax.ppermute(array, AXES, pairs)

    row = swapped(leaving, QUAD)
    held = pltpu.VMEM((QUAD, *shape[0]), F32)
    quad, beside = call(quad_body, [shape, line], *parts, leaving, scratch=[held])
    far = swapped(quad, QUAD)
    arrived = [(0, row)]
    (leaving,) = call(follow_body, [line], row, quad)
    low = moved(leaving, QUAD, QUAD, QUAD)
    high = moved(leaving, QUAD, size, QUAD)
    row = high + low
    arrived.append((1, row))
    end = (octets - 1) * size
    last = moved(early[0], end, -1, 1)
    sources = []
    for octet in range(1, octets - 1):
        (leaving,) = call(octet_exit_body, [((PAD, width), F32)], row, quad, far)
        if octet == octets - 2:
            row = moved(leaving, octet * size, size, size)
        else:
            sources.append((octet, len(arrived)))
            row = swapped(leaving, (octet ^ (octet + 1)) * size)
        arrived.append((octet + 1, row))
    first = moved(early[0], size, -1, 1)
    (prefix,) = call(prefix_body, [shape], *parts, far, leaving, scratch=[held])
    targets, rows = zip(*arrived)
    return call(
        functools.partial(last_body, targets, sources),
        [line, line], *rows, final, beside, far, first + last, prefix,
    )


def solution(mesh):
    return jax.shard_map(
        on_device,
        mesh=mesh,
        in_specs=(
            P(("grp", "seg"), None),
            P(("grp", "seg"), None, None),
            P(),
            P("grp", None),
            P(("grp", "seg"), None),
        ),
        out_specs=(P(("grp", "seg"), None), P(("grp", "seg"), None)),
        check_vma=False,
    )
```

```python
import functools
import jax
import jax.numpy as jnp
from jax import lax
from jax.experimental import pallas as pl
from jax.experimental.pallas import tpu as pltpu
from jax.sharding import PartitionSpec as P


AXES = ("grp", "seg")
PAD = 8
QUAD = 4
VMEM = pl.BlockSpec(memory_space=pltpu.VMEM)
HBM = pl.BlockSpec(memory_space=pltpu.HBM)
F32 = jnp.float32


def halves(a):
    high = a.astype(jnp.bfloat16)
    return high, (a - high.astype(jnp.float32)).astype(jnp.bfloat16)


def dot(a, b, dims=((1,), (0,))):
    def one(x, y):
        return lax.dot_general(
            x, y, (dims, ((), ())), preferred_element_type=jnp.float32
        )

    (ah, al), (bh, bl) = halves(a), halves(b)
    return one(ah, bh) + (one(ah, bl) + one(al, bh))


def times(row, mat):
    n = mat.shape[0]
    on = lax.broadcasted_iota(jnp.int32, (n, n), 0) == lax.broadcasted_iota(
        jnp.int32, (n, n), 1
    )
    column = jnp.sum(jnp.where(on, row, 0.0), axis=1, keepdims=True)
    return jnp.sum(mat * column, axis=0, keepdims=True)


def call(body, shapes, *args, scratch=(), raw=False):
    out = tuple(jax.ShapeDtypeStruct(*s) for s in shapes)
    return pl.pallas_call(
        body,
        out_shape=out,
        in_specs=[HBM if raw else VMEM] * len(args),
        out_specs=tuple(VMEM for _ in out),
        scratch_shapes=list(scratch),
        compiler_params=pltpu.CompilerParams(vmem_limit_bytes=8 << 20),
    )(*args)


def where_am_i():
    return lax.axis_index("grp") * lax.axis_size("seg") + lax.axis_index("seg")


def put_composed(ref, earlier, later):
    width = later.shape[1]
    both = dot(earlier, later[:width])
    ref[:width] = both[:width]
    ref[width:] = both[width:] + later[width:]


def lookup(table, index, base):
    rows, width = table.shape
    level = lax.broadcasted_iota(jnp.int32, (rows, width), 0) + base
    kept = table[...]
    found = [
        jnp.sum(jnp.where(index[k : k + 1, :] == level, kept, 0.0), axis=0, keepdims=True)
        for k in range(index.shape[0])
    ]
    return jnp.concatenate(found, axis=0)


def early_body(
    inv_len, nodes_in, loss_in, jac_in, own_in, index_in,
    nodes, loss, jac, index, near, sens, state, own, sems,
):
    steps, width, _ = jac.shape
    copies = [
        pltpu.make_async_copy(src, dst, sems.at[k])
        for k, (src, dst) in enumerate(
            [(nodes_in, nodes), (loss_in, loss), (jac_in.at[0], jac.at[0])]
            + [(own_in, own), (index_in, index)]
            + [(jac_in.at[pl.ds(1, steps - 1)], jac.at[pl.ds(1, steps - 1)])]
        )
    ]
    for copy in copies:
        copy.start()
    for copy in copies[:3]:
        copy.wait()
    start = jnp.broadcast_to(nodes[...], (PAD, width))
    rates = loss[...]
    slope = jnp.tanh(start)
    weight = inv_len * (rates * (1.0 - slope * slope))
    row = lax.broadcasted_iota(jnp.int32, (width, width), 0)
    col = lax.broadcasted_iota(jnp.int32, (width, width), 1)
    first = jnp.where(row == col, weight[:1], 0.0)
    both = dot(
        jnp.concatenate([first, -inv_len * rates * slope], axis=0), jac[0], ((1,), (1,))
    )
    sens[...] = jnp.where(row == col, 1.0, 0.0) - both[:width]
    state[...] = start + both[width:]
    for copy in copies[3:5]:
        copy.wait()
    near[...] = lookup(own, index, lax.axis_index("grp") * own.shape[0])
    copies[5].wait()


def local_body(
    inv_len, src_scale, other, nodes, loss, jac, index, near, sens_in, state_in,
    top, bottom, final,
):
    steps, width, _ = jac.shape
    cut = top.shape[0]
    rows = other.shape[0]
    source = near[...] + lookup(other, index, (1 - lax.axis_index("grp")) * rows)
    rates = loss[...]
    sens = sens_in[...]
    spread = jnp.sum(jac[0] * (src_scale * source[:1]), axis=1, keepdims=True)
    on = lax.broadcasted_iota(jnp.int32, (width, width), 0) == lax.broadcasted_iota(
        jnp.int32, (width, width), 1
    )
    state = state_in[...] + jnp.sum(jnp.where(on, spread, 0.0), axis=0, keepdims=True)
    for step in range(1, steps):
        slope = jnp.tanh(state)
        weight = inv_len * (rates * (1.0 - slope * slope))
        drive = src_scale * source[step : step + 1] - inv_len * rates * slope
        both = dot(
            jnp.concatenate([sens * weight[:1], drive], axis=0), jac[step], ((1,), (1,))
        )
        sens = sens - both[:width]
        state = state + both[width:]
    sens = jnp.where(where_am_i() == 0, 0.0, sens)
    top[...] = sens[:cut]
    bottom[: width - cut] = sens[cut:]
    offset = state - jnp.broadcast_to(times(nodes[...], sens), state.shape)
    bottom[width - cut :] = offset
    bottom[width - cut + 1 : width - cut + 2] = nodes[...]
    final[...] = state[:1]


def in_order(held, parts):
    member = lax.rem(where_am_i(), QUAD)
    cut = parts[0].shape[0]
    for k in range(QUAD):
        place = jnp.bitwise_xor(member, k)
        held[place, :cut] = parts[2 * k][...]
        held[place, cut:] = parts[2 * k + 1][...]


def follow(entry, mapping):
    width = mapping.shape[1]
    return times(entry, mapping[:width]) + mapping[width : width + 1]


def first_exit_body(*refs):
    *parts, leaving = refs
    place = where_am_i()
    width = leaving.shape[1]
    cut = parts[0].shape[0]

    def step(state, k):
        upper, lower = parts[2 * k : 2 * k + 2]
        rest = width - cut
        n = lax.broadcasted_iota(jnp.int32, (width, width), 0)
        on = n == lax.broadcasted_iota(jnp.int32, (width, width), 1)
        column = jnp.sum(jnp.where(on, state, 0.0), axis=1, keepdims=True)
        return (
            jnp.sum(upper[...] * column[:cut], axis=0, keepdims=True)
            + jnp.sum(lower[:rest] * column[cut:], axis=0, keepdims=True)
            + lower[rest : rest + 1]
        )

    leaving[...] = jnp.zeros_like(leaving)
    for member in range(QUAD):

        @pl.when(lax.rem(place, QUAD) == member)
        def _():
            node = width - cut + 1
            leaving[1:2] = parts[2 * member + 1][node : node + 1]

        @pl.when(place == member)
        def _():
            state = parts[2 * member + 1][width - cut : width - cut + 1]
            for k in range(1, QUAD):
                state = step(state, member ^ k)
            leaving[:1] = state


def quad_body(*refs):
    *parts, after, total, beside, held = refs
    width = total.shape[1]
    in_order(held, parts)
    member = lax.rem(where_am_i(), QUAD)
    node = width + 1
    beside[...] = held[lax.rem(member + 1, QUAD), node : node + 1]

    @pl.when(where_am_i() < QUAD)
    def _():
        total[...] = jnp.zeros_like(total)

    @pl.when(where_am_i() >= QUAD)
    def _():
        head = held[0, node : node + 1]
        put_composed(total, held[0], held[1])
        put_composed(held.at[0], held[2], held[3])
        put_composed(total, total[...], held[0])
        total[node : node + 1] = head


def is_upper():
    return lax.rem(lax.div(where_am_i(), QUAD), 2) == 1


def is_last():
    count = lax.axis_size("grp") * lax.axis_size("seg")
    return where_am_i() >= count - 2 * QUAD


def prefix_body(*refs):
    *parts, far, late, after, prefix, held = refs
    in_order(held, parts)
    member = lax.rem(where_am_i(), QUAD)
    prefix[...] = held[0]

    @pl.when(is_upper() & jnp.logical_not(is_last()) & (where_am_i() >= 2 * QUAD))
    def _():
        put_composed(prefix, far[...], held[0])

    @pl.when(is_upper() & is_last())
    def _():
        put_composed(prefix, late[...], held[0])

    for k in range(1, QUAD):

        @pl.when(member >= k)
        def _():
            put_composed(prefix, prefix[...], held[k])


def quad_exit_body(entry, mapping, out):
    width = mapping.shape[1]
    out[...] = jnp.zeros_like(out)
    out[:1] = follow(entry[:1], mapping[...])
    out[1:2] = mapping[width + 1 : width + 2]


def octet_exit_body(low, high, own, far, out):
    upper = is_upper()
    width = own.shape[1]
    out[...] = jnp.zeros_like(out)

    @pl.when(upper)
    def _():
        out[:1] = follow(follow(high[:1], far[...]), own[...])
        out[1:2] = far[width + 1 : width + 2]

    @pl.when(jnp.logical_not(upper))
    def _():
        out[:1] = follow(follow(low[:1], own[...]), far[...])
        out[1:2] = own[width + 1 : width + 2]


def last_body(entries, backs, count, *refs):
    rows = refs[:count]
    final, beside, far, late, mapping, out, defect = refs[count:]
    place = where_am_i()
    width = out.shape[1]
    end = lax.rem(place, QUAD) == QUAD - 1
    quad = lax.div(place, QUAD)
    entry = jnp.zeros_like(out)
    for target, k in entries:
        entry = jnp.where(quad == target, rows[k][:1], entry)
    node = slice(width + 1, width + 2)
    following = jnp.where(is_last(), late[node], far[node])
    following = jnp.where(is_upper(), 0.0, following)
    for target, k in backs:
        following = jnp.where(quad == target, rows[k][1:2], following)
    following = jnp.where(end, following, beside[...])
    out[...] = follow(entry, mapping[...])
    defect[...] = final[...] - following


def on_device(nodes, jac_inverse, loss_rates, rate_table, rate_index):
    steps, width, _ = jac_inverse.shape
    seg_count = lax.axis_size("seg")
    segments = lax.axis_size("grp") * seg_count
    inv_len = 1.0 / (steps * segments)
    src_scale = 0.25 / steps

    def swapped(array, by):
        return lax.ppermute(array, AXES, [(i, i ^ by) for i in range(segments)])

    other = swapped(rate_table, seg_count)
    shape = ((width + PAD, width), F32)
    line = ((1, width), F32)
    early = call(
        functools.partial(early_body, inv_len),
        [
            line, line, (jac_inverse.shape, F32), (rate_index.shape, jnp.int32),
            ((steps, width), F32), ((width, width), F32), ((PAD, width), F32),
        ],
        *(
            pltpu.with_memory_space_constraint(array, pltpu.HBM)
            for array in (nodes, loss_rates[None], jac_inverse, rate_table, rate_index)
        ),
        scratch=[pltpu.VMEM(rate_table.shape, F32), pltpu.SemaphoreType.DMA((6,))],
        raw=True,
    )
    cut = width // 2
    halves = [((cut, width), F32), ((width - cut + PAD, width), F32)]
    top, bottom, final = call(
        functools.partial(local_body, inv_len, src_scale),
        [*halves, line], other, *early,
    )
    top1 = swapped(top, 1)
    bottom2 = swapped(bottom, 2)
    bottom1 = swapped(bottom, 1)
    top2 = swapped(top, 2)
    top3 = swapped(top1, 2)
    bottom3 = swapped(bottom2, 1)
    parts = [top, bottom, top1, bottom1, top2, bottom2, top3, bottom3]
    wide = ((PAD, width), F32)
    held = pltpu.VMEM((QUAD, *shape[0]), F32)
    octets = segments // (2 * QUAD)

    def quads_swapped(array, quad_pairs):
        to = {}
        for one, two in quad_pairs:
            for k in range(QUAD):
                to[one * QUAD + k] = two * QUAD + k
                to[two * QUAD + k] = one * QUAD + k
        busy = set(to)
        for i in range(segments):
            if i not in busy:
                core = (i + seg_count) % segments
                to[i] = i ^ 1 if core in busy else core
        return lax.ppermute(array, AXES, sorted(to.items()))

    (leaving,) = call(first_exit_body, [wide], *parts)
    rows, entries, backs = [], [], []

    row = quads_swapped(leaving, [(0, 1)])
    rows.append(row)
    entries.append((1, 0))
    backs.append((0, 0))
    quad, beside = call(quad_body, [shape, line], *parts, leaving, scratch=[held])
    far = quads_swapped(quad, [(2 * o, 2 * o + 1) for o in range(1, octets - 1)])

    (leaving,) = call(quad_exit_body, [wide], row, quad)
    end = 2 * octets - 2
    high = quads_swapped(leaving, [(1, 3), (end - 1, end)])
    low = quads_swapped(leaving, [(1, 2)])
    rows.extend((high, low))
    entries.extend(((3, 1), (2, 2)))
    backs.extend(((end - 1, 1), (1, 2)))
    first = segments - 2 * QUAD
    for octet in range(1, octets - 1):
        (leaving,) = call(octet_exit_body, [wide], low, high, quad, far)
        source = 2 * octet
        if octet == octets - 2:
            pairs = [(i, i + 2 * QUAD) for i in range(first - 2 * QUAD, first)]
            late = quads_swapped(quad, [(end, end + 1)])
            low = lax.ppermute(leaving, AXES, pairs)
        else:
            pairs = [(source, source + 2), (source + 1, source + 3)]
            low = high = quads_swapped(leaving, pairs)
            backs.append((source + 1, len(rows)))
        entries.append((source + 2, len(rows)))
        entries.append((source + 3, len(rows)))
        rows.append(low)
    (prefix,) = call(
        prefix_body, [shape], *parts, far, late, leaving, scratch=[held]
    )
    return call(
        functools.partial(last_body, entries, backs, len(rows)),
        [line, line], *rows, final, beside, far, late, prefix,
    )


def solution(mesh):
    return jax.shard_map(
        on_device,
        mesh=mesh,
        in_specs=(
            P(("grp", "seg"), None),
            P(("grp", "seg"), None, None),
            P(),
            P("grp", None),
            P(("grp", "seg"), None),
        ),
        out_specs=(P(("grp", "seg"), None), P(("grp", "seg"), None)),
        check_vma=False,
    )
```

```python
import functools
import jax
import jax.numpy as jnp
from jax import lax
from jax.experimental import pallas as pl
from jax.experimental.pallas import tpu as pltpu
from jax.sharding import PartitionSpec as P


AXES = ("grp", "seg")
PAD = 8
QUAD = 4
VMEM = pl.BlockSpec(memory_space=pltpu.VMEM)
HBM = pl.BlockSpec(memory_space=pltpu.HBM)
F32 = jnp.float32


def halves(a):
    high = a.astype(jnp.bfloat16)
    return high, (a - high.astype(jnp.float32)).astype(jnp.bfloat16)


def dot(a, b, dims=((1,), (0,))):
    def one(x, y):
        return lax.dot_general(
            x, y, (dims, ((), ())), preferred_element_type=jnp.float32
        )

    (ah, al), (bh, bl) = halves(a), halves(b)
    return one(ah, bh) + (one(ah, bl) + one(al, bh))


def times(row, mat):
    n = mat.shape[0]
    on = lax.broadcasted_iota(jnp.int32, (n, n), 0) == lax.broadcasted_iota(
        jnp.int32, (n, n), 1
    )
    column = jnp.sum(jnp.where(on, row, 0.0), axis=1, keepdims=True)
    return jnp.sum(mat * column, axis=0, keepdims=True)


def call(body, shapes, *args, scratch=(), raw=False):
    out = tuple(jax.ShapeDtypeStruct(*s) for s in shapes)
    return pl.pallas_call(
        body,
        out_shape=out,
        in_specs=[HBM if raw else VMEM] * len(args),
        out_specs=tuple(VMEM for _ in out),
        scratch_shapes=list(scratch),
        compiler_params=pltpu.CompilerParams(vmem_limit_bytes=8 << 20),
    )(*args)


def where_am_i():
    return lax.axis_index("grp") * lax.axis_size("seg") + lax.axis_index("seg")


def put_composed(ref, earlier, later):
    width = later.shape[1]
    both = dot(earlier, later[:width])
    ref[:width] = both[:width]
    ref[width:] = both[width:] + later[width:]


def lookup(table, index, base):
    rows, width = table.shape
    level = lax.broadcasted_iota(jnp.int32, (rows, width), 0) + base
    kept = table[...]
    found = [
        jnp.sum(jnp.where(index[k : k + 1, :] == level, kept, 0.0), axis=0, keepdims=True)
        for k in range(index.shape[0])
    ]
    return jnp.concatenate(found, axis=0)


def early_body(
    inv_len, nodes_in, loss_in, jac_in, own_in, index_in,
    nodes, loss, jac, index, near, sens, state, own, sems,
):
    steps, width, _ = jac.shape
    pairs = [(index_in, index), (own_in, own), (nodes_in, nodes), (loss_in, loss)]
    pairs += [(jac_in.at[k], jac.at[k]) for k in range(steps)]
    copies = [
        pltpu.make_async_copy(src, dst, sems.at[k]) for k, (src, dst) in enumerate(pairs)
    ]
    for copy in copies:
        copy.start()
    for copy in copies[:4]:
        copy.wait()
    near[...] = lookup(own, index, lax.axis_index("grp") * own.shape[0])
    start = jnp.broadcast_to(nodes[...], (PAD, width))
    rates = loss[...]
    slope = jnp.tanh(start)
    weight = inv_len * (rates * (1.0 - slope * slope))
    row = lax.broadcasted_iota(jnp.int32, (width, width), 0)
    col = lax.broadcasted_iota(jnp.int32, (width, width), 1)
    first = jnp.where(row == col, weight[:1], 0.0)
    copies[4].wait()
    both = dot(
        jnp.concatenate([first, -inv_len * rates * slope], axis=0), jac[0], ((1,), (1,))
    )
    sens[...] = jnp.where(row == col, 1.0, 0.0) - both[:width]
    state[...] = start + both[width:]
    for copy in copies[5:]:
        copy.wait()


def local_body(
    inv_len, src_scale, other, nodes, loss, jac, index, near, sens_in, state_in,
    top, bottom, final,
):
    steps, width, _ = jac.shape
    cut = top.shape[0]
    rows = other.shape[0]
    source = near[...] + lookup(other, index, (1 - lax.axis_index("grp")) * rows)
    rates = loss[...]
    sens = sens_in[...]
    spread = jnp.sum(jac[0] * (src_scale * source[:1]), axis=1, keepdims=True)
    on = lax.broadcasted_iota(jnp.int32, (width, width), 0) == lax.broadcasted_iota(
        jnp.int32, (width, width), 1
    )
    state = state_in[...] + jnp.sum(jnp.where(on, spread, 0.0), axis=0, keepdims=True)
    for step in range(1, steps):
        slope = jnp.tanh(state)
        weight = inv_len * (rates * (1.0 - slope * slope))
        drive = src_scale * source[step : step + 1] - inv_len * rates * slope
        both = dot(
            jnp.concatenate([sens * weight[:1], drive], axis=0), jac[step], ((1,), (1,))
        )
        sens = sens - both[:width]
        state = state + both[width:]
    sens = jnp.where(where_am_i() == 0, 0.0, sens)
    top[...] = sens[:cut]
    bottom[: width - cut] = sens[cut:]
    offset = state - jnp.broadcast_to(times(nodes[...], sens), state.shape)
    bottom[width - cut :] = offset
    bottom[width - cut + 1 : width - cut + 2] = nodes[...]
    final[...] = state[:1]


def in_order(held, parts):
    member = lax.rem(where_am_i(), QUAD)
    cut = parts[0].shape[0]
    for k in range(QUAD):
        place = jnp.bitwise_xor(member, k)
        held[place, :cut] = parts[2 * k][...]
        held[place, cut:] = parts[2 * k + 1][...]


def follow(entry, mapping):
    width = mapping.shape[1]
    return times(entry, mapping[:width]) + mapping[width : width + 1]


def first_exit_body(*refs):
    *parts, leaving = refs
    place = where_am_i()
    width = leaving.shape[1]
    cut = parts[0].shape[0]

    def step(state, k):
        upper, lower = parts[2 * k : 2 * k + 2]
        rest = width - cut
        n = lax.broadcasted_iota(jnp.int32, (width, width), 0)
        on = n == lax.broadcasted_iota(jnp.int32, (width, width), 1)
        column = jnp.sum(jnp.where(on, state, 0.0), axis=1, keepdims=True)
        return (
            jnp.sum(upper[...] * column[:cut], axis=0, keepdims=True)
            + jnp.sum(lower[:rest] * column[cut:], axis=0, keepdims=True)
            + lower[rest : rest + 1]
        )

    leaving[...] = jnp.zeros_like(leaving)
    for member in range(QUAD):

        @pl.when(lax.rem(place, QUAD) == member)
        def _():
            node = width - cut + 1
            leaving[1:2] = parts[2 * member + 1][node : node + 1]

        @pl.when(place == member)
        def _():
            state = parts[2 * member + 1][width - cut : width - cut + 1]
            for k in range(1, QUAD):
                state = step(state, member ^ k)
            leaving[:1] = state


def quad_body(*refs):
    *parts, after, total, beside, held = refs
    width = total.shape[1]
    in_order(held, parts)
    member = lax.rem(where_am_i(), QUAD)
    node = width + 1
    beside[...] = held[lax.rem(member + 1, QUAD), node : node + 1]

    @pl.when(where_am_i() < QUAD)
    def _():
        total[...] = jnp.zeros_like(total)

    @pl.when(where_am_i() >= QUAD)
    def _():
        head = held[0, node : node + 1]
        put_composed(total, held[0], held[1])
        put_composed(held.at[0], held[2], held[3])
        put_composed(total, total[...], held[0])
        total[node : node + 1] = head


def is_upper():
    return lax.rem(lax.div(where_am_i(), QUAD), 2) == 1


def is_last():
    count = lax.axis_size("grp") * lax.axis_size("seg")
    return where_am_i() >= count - 2 * QUAD


def prefix_body(*refs):
    *parts, far, late, after, prefix, held = refs
    in_order(held, parts)
    member = lax.rem(where_am_i(), QUAD)
    prefix[...] = held[0]

    @pl.when(is_upper() & jnp.logical_not(is_last()) & (where_am_i() >= 2 * QUAD))
    def _():
        put_composed(prefix, far[...], held[0])

    @pl.when(is_upper() & is_last())
    def _():
        put_composed(prefix, late[...], held[0])

    for k in range(1, QUAD):

        @pl.when(member >= k)
        def _():
            put_composed(prefix, prefix[...], held[k])


def quad_exit_body(entry, mapping, out):
    width = mapping.shape[1]
    out[...] = jnp.zeros_like(out)
    out[:1] = follow(entry[:1], mapping[...])
    out[1:2] = mapping[width + 1 : width + 2]


def octet_exit_body(low, high, own, far, out):
    upper = is_upper()
    width = own.shape[1]
    out[...] = jnp.zeros_like(out)

    @pl.when(upper)
    def _():
        out[:1] = follow(follow(high[:1], far[...]), own[...])
        out[1:2] = far[width + 1 : width + 2]

    @pl.when(jnp.logical_not(upper))
    def _():
        out[:1] = follow(follow(low[:1], own[...]), far[...])
        out[1:2] = own[width + 1 : width + 2]


def last_body(entries, backs, count, *refs):
    rows = refs[:count]
    final, beside, far, late, mapping, out, defect = refs[count:]
    place = where_am_i()
    width = out.shape[1]
    end = lax.rem(place, QUAD) == QUAD - 1
    quad = lax.div(place, QUAD)
    entry = jnp.zeros_like(out)
    for target, k in entries:
        entry = jnp.where(quad == target, rows[k][:1], entry)
    node = slice(width + 1, width + 2)
    following = jnp.where(is_last(), late[node], far[node])
    following = jnp.where(is_upper(), 0.0, following)
    for target, k in backs:
        following = jnp.where(quad == target, rows[k][1:2], following)
    following = jnp.where(end, following, beside[...])
    out[...] = follow(entry, mapping[...])
    defect[...] = final[...] - following


def on_device(nodes, jac_inverse, loss_rates, rate_table, rate_index):
    steps, width, _ = jac_inverse.shape
    seg_count = lax.axis_size("seg")
    segments = lax.axis_size("grp") * seg_count
    inv_len = 1.0 / (steps * segments)
    src_scale = 0.25 / steps

    def swapped(array, by):
        return lax.ppermute(array, AXES, [(i, i ^ by) for i in range(segments)])

    other = swapped(rate_table, seg_count)
    shape = ((width + PAD, width), F32)
    line = ((1, width), F32)
    early = call(
        functools.partial(early_body, inv_len),
        [
            line, line, (jac_inverse.shape, F32), (rate_index.shape, jnp.int32),
            ((steps, width), F32), ((width, width), F32), ((PAD, width), F32),
        ],
        *(
            pltpu.with_memory_space_constraint(array, pltpu.HBM)
            for array in (nodes, loss_rates[None], jac_inverse, rate_table, rate_index)
        ),
        scratch=[pltpu.VMEM(rate_table.shape, F32), pltpu.SemaphoreType.DMA((4 + steps,))],
        raw=True,
    )
    cut = width // 2
    halves = [((cut, width), F32), ((width - cut + PAD, width), F32)]
    top, bottom, final = call(
        functools.partial(local_body, inv_len, src_scale),
        [*halves, line], other, *early,
    )
    top1 = swapped(top, 1)
    bottom2 = swapped(bottom, 2)
    bottom1 = swapped(bottom, 1)
    top2 = swapped(top, 2)
    top3 = swapped(top1, 2)
    bottom3 = swapped(bottom2, 1)
    parts = [top, bottom, top1, bottom1, top2, bottom2, top3, bottom3]
    wide = ((2, width), F32)
    held = pltpu.VMEM((QUAD, *shape[0]), F32)
    octets = segments // (2 * QUAD)

    def quads_swapped(array, quad_pairs):
        to = {}
        for one, two in quad_pairs:
            for k in range(QUAD):
                to[one * QUAD + k] = two * QUAD + k
                to[two * QUAD + k] = one * QUAD + k
        busy = set(to)
        for i in range(segments):
            if i not in busy:
                core = (i + seg_count) % segments
                to[i] = i ^ 1 if core in busy else core
        return lax.ppermute(array, AXES, sorted(to.items()))

    (leaving,) = call(first_exit_body, [wide], *parts)
    rows, entries, backs = [], [], []

    row = quads_swapped(leaving, [(0, 1)])
    rows.append(row)
    entries.append((1, 0))
    backs.append((0, 0))
    quad, beside = call(quad_body, [shape, line], *parts, leaving, scratch=[held])
    far = quads_swapped(quad, [(2 * o, 2 * o + 1) for o in range(1, octets - 1)])

    (leaving,) = call(quad_exit_body, [wide], row, quad)
    end = 2 * octets - 2
    high = quads_swapped(leaving, [(1, 3)])
    low = quads_swapped(leaving, [(1, 2), (end - 1, end)])
    rows.extend((high, low))
    entries.extend(((3, 1), (2, 2)))
    backs.extend(((end - 1, 2), (1, 2)))
    first = segments - 2 * QUAD
    for octet in range(1, octets - 1):
        (leaving,) = call(octet_exit_body, [wide], low, high, quad, far)
        source = 2 * octet
        if octet == octets - 2:
            pairs = [(i, i + 2 * QUAD) for i in range(first - 2 * QUAD, first)]
            late = quads_swapped(quad, [(end, end + 1)])
            low = lax.ppermute(leaving, AXES, pairs)
        else:
            pairs = [(source, source + 2), (source + 1, source + 3)]
            low = high = quads_swapped(leaving, pairs)
            backs.append((source + 1, len(rows)))
        entries.append((source + 2, len(rows)))
        entries.append((source + 3, len(rows)))
        rows.append(low)
    (prefix,) = call(
        prefix_body, [shape], *parts, far, late, leaving, scratch=[held]
    )
    return call(
        functools.partial(last_body, entries, backs, len(rows)),
        [line, line], *rows, final, beside, far, late, prefix,
    )


def solution(mesh):
    return jax.shard_map(
        on_device,
        mesh=mesh,
        in_specs=(
            P(("grp", "seg"), None),
            P(("grp", "seg"), None, None),
            P(),
            P("grp", None),
            P(("grp", "seg"), None),
        ),
        out_specs=(P(("grp", "seg"), None), P(("grp", "seg"), None)),
        check_vma=False,
    )
```

```python
import functools
import jax
import jax.numpy as jnp
from jax import lax
from jax.experimental import pallas as pl
from jax.experimental.pallas import tpu as pltpu
from jax.sharding import PartitionSpec as P


AXES = ("grp", "seg")
PAD = 8
QUAD = 4
VMEM = pl.BlockSpec(memory_space=pltpu.VMEM)
HBM = pl.BlockSpec(memory_space=pltpu.HBM)
F32 = jnp.float32


def halves(a):
    high = a.astype(jnp.bfloat16)
    return high, (a - high.astype(jnp.float32)).astype(jnp.bfloat16)


def dot(a, b, dims=((1,), (0,))):
    def one(x, y):
        return lax.dot_general(
            x, y, (dims, ((), ())), preferred_element_type=jnp.float32
        )

    (ah, al), (bh, bl) = halves(a), halves(b)
    return one(ah, bh) + (one(ah, bl) + one(al, bh))


def times(row, mat):
    n = mat.shape[0]
    on = lax.broadcasted_iota(jnp.int32, (n, n), 0) == lax.broadcasted_iota(
        jnp.int32, (n, n), 1
    )
    column = jnp.sum(jnp.where(on, row, 0.0), axis=1, keepdims=True)
    return jnp.sum(mat * column, axis=0, keepdims=True)


def call(body, shapes, *args, scratch=(), raw=False):
    out = tuple(jax.ShapeDtypeStruct(*s) for s in shapes)
    return pl.pallas_call(
        body,
        out_shape=out,
        in_specs=[HBM if raw else VMEM] * len(args),
        out_specs=tuple(VMEM for _ in out),
        scratch_shapes=list(scratch),
        compiler_params=pltpu.CompilerParams(vmem_limit_bytes=8 << 20),
    )(*args)


def where_am_i():
    return lax.axis_index("grp") * lax.axis_size("seg") + lax.axis_index("seg")


def put_composed(ref, earlier, later):
    width = later.shape[1]
    both = dot(earlier, later[:width])
    ref[:width] = both[:width]
    ref[width:] = both[width:] + later[width:]


def lookup(table, index, base):
    rows, width = table.shape
    level = lax.broadcasted_iota(jnp.int32, (rows, width), 0) + base
    kept = table[...]
    found = [
        jnp.sum(jnp.where(index[k : k + 1, :] == level, kept, 0.0), axis=0, keepdims=True)
        for k in range(index.shape[0])
    ]
    return jnp.concatenate(found, axis=0)


def early_body(
    inv_len, nodes_in, loss_in, jac_in, own_in, index_in,
    nodes, loss, jac, index, near, sens, state, own, sems,
):
    steps, width, _ = jac.shape
    pairs = [(index_in, index), (own_in, own), (nodes_in, nodes), (loss_in, loss)]
    pairs += [(jac_in.at[k], jac.at[k]) for k in range(steps)]
    copies = [
        pltpu.make_async_copy(src, dst, sems.at[k]) for k, (src, dst) in enumerate(pairs)
    ]
    for copy in copies:
        copy.start()
    for copy in copies[:4]:
        copy.wait()
    near[...] = lookup(own, index, lax.axis_index("grp") * own.shape[0])
    start = jnp.broadcast_to(nodes[...], (PAD, width))
    rates = loss[...]
    slope = jnp.tanh(start)
    weight = inv_len * (rates * (1.0 - slope * slope))
    row = lax.broadcasted_iota(jnp.int32, (width, width), 0)
    col = lax.broadcasted_iota(jnp.int32, (width, width), 1)
    first = jnp.where(row == col, weight[:1], 0.0)
    copies[4].wait()
    both = dot(
        jnp.concatenate([first, -inv_len * rates * slope], axis=0), jac[0], ((1,), (1,))
    )
    sens[...] = jnp.where(row == col, 1.0, 0.0) - both[:width]
    state[...] = start + both[width:]
    for copy in copies[5:]:
        copy.wait()


def local_body(
    inv_len, src_scale, other, nodes, loss, jac, index, near, sens_in, state_in,
    top, bottom, final,
):
    steps, width, _ = jac.shape
    cut = top.shape[0]
    rows = other.shape[0]
    source = near[...] + lookup(other, index, (1 - lax.axis_index("grp")) * rows)
    rates = loss[...]
    sens = sens_in[...]
    spread = jnp.sum(jac[0] * (src_scale * source[:1]), axis=1, keepdims=True)
    on = lax.broadcasted_iota(jnp.int32, (width, width), 0) == lax.broadcasted_iota(
        jnp.int32, (width, width), 1
    )
    state = state_in[...] + jnp.sum(jnp.where(on, spread, 0.0), axis=0, keepdims=True)
    for step in range(1, steps):
        slope = jnp.tanh(state)
        weight = inv_len * (rates * (1.0 - slope * slope))
        drive = src_scale * source[step : step + 1] - inv_len * rates * slope
        both = dot(
            jnp.concatenate([sens * weight[:1], drive], axis=0), jac[step], ((1,), (1,))
        )
        sens = sens - both[:width]
        state = state + both[width:]
    sens = jnp.where(where_am_i() == 0, 0.0, sens)
    top[...] = sens[:cut]
    bottom[: width - cut] = sens[cut:]
    offset = state - jnp.broadcast_to(times(nodes[...], sens), state.shape)
    bottom[width - cut :] = offset
    bottom[width - cut + 1 : width - cut + 2] = nodes[...]
    final[...] = state[:1]


def in_order(held, parts):
    member = lax.rem(where_am_i(), QUAD)
    cut = parts[0].shape[0]
    for k in range(QUAD):
        place = jnp.bitwise_xor(member, k)
        held[place, :cut] = parts[2 * k][...]
        held[place, cut:] = parts[2 * k + 1][...]


def follow(entry, mapping):
    width = mapping.shape[1]
    return times(entry, mapping[:width]) + mapping[width : width + 1]


def first_exit_body(*refs):
    *parts, leaving = refs
    place = where_am_i()
    width = leaving.shape[1]
    cut = parts[0].shape[0]

    def step(state, k):
        upper, lower = parts[2 * k : 2 * k + 2]
        rest = width - cut
        n = lax.broadcasted_iota(jnp.int32, (width, width), 0)
        on = n == lax.broadcasted_iota(jnp.int32, (width, width), 1)
        column = jnp.sum(jnp.where(on, state, 0.0), axis=1, keepdims=True)
        return (
            jnp.sum(upper[...] * column[:cut], axis=0, keepdims=True)
            + jnp.sum(lower[:rest] * column[cut:], axis=0, keepdims=True)
            + lower[rest : rest + 1]
        )

    leaving[...] = jnp.zeros_like(leaving)
    for member in range(QUAD):

        @pl.when(lax.rem(place, QUAD) == member)
        def _():
            node = width - cut + 1
            leaving[1:2] = parts[2 * member + 1][node : node + 1]

        @pl.when(place == member)
        def _():
            state = parts[2 * member + 1][width - cut : width - cut + 1]
            for k in range(1, QUAD):
                state = step(state, member ^ k)
            leaving[:1] = state


def join(ref, k, top, bottom):
    cut = top.shape[0]
    ref[k, :cut] = top[...]
    ref[k, cut:] = bottom[...]


def pair_body(top, bottom, top1, bottom1, total, held):
    width = total.shape[1]
    node = slice(width + 1, width + 2)
    side = lax.rem(where_am_i(), 2)
    join(held, side, top, bottom)
    join(held, 1 - side, top1, bottom1)
    put_composed(total, held[0], held[1])
    total[node] = held[0, node]


def quad_body(pair, bottom1, top2, bottom2, top3, bottom3, total, beside, held):
    width = total.shape[1]
    node = slice(width + 1, width + 2)
    side = lax.rem(where_am_i(), 2)
    upper = lax.rem(lax.div(where_am_i(), 2), 2) == 1
    join(held, side, top2, bottom2)
    join(held, 1 - side, top3, bottom3)
    end = bottom1.shape[0] - PAD + 1
    near, far = bottom1[end : end + 1], bottom3[end : end + 1]
    beside[...] = jnp.where(side == 0, near, far)

    @pl.when(where_am_i() < QUAD)
    def _():
        total[...] = jnp.zeros_like(total)

    @pl.when(where_am_i() >= QUAD)
    def _():
        head = jnp.where(upper, held[0, node], pair[node])
        put_composed(held.at[2], held[0], held[1])

        @pl.when(upper)
        def _():
            put_composed(total, held[2], pair[...])

        @pl.when(jnp.logical_not(upper))
        def _():
            put_composed(total, pair[...], held[2])

        total[node] = head


def is_upper():
    return lax.rem(lax.div(where_am_i(), QUAD), 2) == 1


def is_last():
    count = lax.axis_size("grp") * lax.axis_size("seg")
    return where_am_i() >= count - 2 * QUAD


def prefix_body(*refs):
    *parts, far, late, after, prefix, held = refs
    in_order(held, parts)
    member = lax.rem(where_am_i(), QUAD)
    prefix[...] = held[0]

    @pl.when(is_upper() & jnp.logical_not(is_last()) & (where_am_i() >= 2 * QUAD))
    def _():
        put_composed(prefix, far[...], held[0])

    @pl.when(is_upper() & is_last())
    def _():
        put_composed(prefix, late[...], held[0])

    for k in range(1, QUAD):

        @pl.when(member >= k)
        def _():
            put_composed(prefix, prefix[...], held[k])


def quad_exit_body(entry, mapping, out):
    width = mapping.shape[1]
    out[...] = jnp.zeros_like(out)
    out[:1] = follow(entry[:1], mapping[...])
    out[1:2] = mapping[width + 1 : width + 2]


def octet_exit_body(low, high, own, far, out):
    upper = is_upper()
    width = own.shape[1]
    out[...] = jnp.zeros_like(out)

    @pl.when(upper)
    def _():
        out[:1] = follow(follow(high[:1], far[...]), own[...])
        out[1:2] = far[width + 1 : width + 2]

    @pl.when(jnp.logical_not(upper))
    def _():
        out[:1] = follow(follow(low[:1], own[...]), far[...])
        out[1:2] = own[width + 1 : width + 2]


def last_body(entries, backs, count, *refs):
    rows = refs[:count]
    final, beside, far, late, mapping, out, defect = refs[count:]
    place = where_am_i()
    width = out.shape[1]
    end = lax.rem(place, QUAD) == QUAD - 1
    quad = lax.div(place, QUAD)
    entry = jnp.zeros_like(out)
    for target, k in entries:
        entry = jnp.where(quad == target, rows[k][:1], entry)
    node = slice(width + 1, width + 2)
    following = jnp.where(is_last(), late[node], far[node])
    following = jnp.where(is_upper(), 0.0, following)
    for target, k in backs:
        following = jnp.where(quad == target, rows[k][1:2], following)
    following = jnp.where(end, following, beside[...])
    out[...] = follow(entry, mapping[...])
    defect[...] = final[...] - following


def on_device(nodes, jac_inverse, loss_rates, rate_table, rate_index):
    steps, width, _ = jac_inverse.shape
    seg_count = lax.axis_size("seg")
    segments = lax.axis_size("grp") * seg_count
    inv_len = 1.0 / (steps * segments)
    src_scale = 0.25 / steps

    def swapped(array, by):
        return lax.ppermute(array, AXES, [(i, i ^ by) for i in range(segments)])

    other = swapped(rate_table, seg_count)
    shape = ((width + PAD, width), F32)
    line = ((1, width), F32)
    early = call(
        functools.partial(early_body, inv_len),
        [
            line, line, (jac_inverse.shape, F32), (rate_index.shape, jnp.int32),
            ((steps, width), F32), ((width, width), F32), ((PAD, width), F32),
        ],
        *(
            pltpu.with_memory_space_constraint(array, pltpu.HBM)
            for array in (nodes, loss_rates[None], jac_inverse, rate_table, rate_index)
        ),
        scratch=[pltpu.VMEM(rate_table.shape, F32), pltpu.SemaphoreType.DMA((4 + steps,))],
        raw=True,
    )
    cut = width // 2
    halves = [((cut, width), F32), ((width - cut + PAD, width), F32)]
    top, bottom, final = call(
        functools.partial(local_body, inv_len, src_scale),
        [*halves, line], other, *early,
    )
    top1 = swapped(top, 1)
    bottom2 = swapped(bottom, 2)
    bottom1 = swapped(bottom, 1)
    top2 = swapped(top, 2)
    top3 = swapped(top1, 2)
    bottom3 = swapped(bottom2, 1)
    parts = [top, bottom, top1, bottom1, top2, bottom2, top3, bottom3]
    wide = ((2, width), F32)
    held = pltpu.VMEM((QUAD, *shape[0]), F32)
    octets = segments // (2 * QUAD)

    def quads_swapped(array, quad_pairs):
        to = {}
        for one, two in quad_pairs:
            for k in range(QUAD):
                to[one * QUAD + k] = two * QUAD + k
                to[two * QUAD + k] = one * QUAD + k
        busy = set(to)
        for i in range(segments):
            if i not in busy:
                core = (i + seg_count) % segments
                to[i] = i ^ 1 if core in busy else core
        return lax.ppermute(array, AXES, sorted(to.items()))

    (leaving,) = call(first_exit_body, [wide], *parts)
    rows, entries, backs = [], [], []

    row = quads_swapped(leaving, [(0, 1)])
    rows.append(row)
    entries.append((1, 0))
    backs.append((0, 0))
    (pair,) = call(pair_body, [shape], *parts[:4], scratch=[held])
    quad, beside = call(
        quad_body, [shape, line], pair, bottom1, top2, bottom2, top3, bottom3, scratch=[held]
    )
    far = quads_swapped(quad, [(2 * o, 2 * o + 1) for o in range(1, octets - 1)])

    (leaving,) = call(quad_exit_body, [wide], row, quad)
    end = 2 * octets - 2
    high = quads_swapped(leaving, [(1, 3)])
    low = quads_swapped(leaving, [(1, 2), (end - 1, end)])
    rows.extend((high, low))
    entries.extend(((3, 1), (2, 2)))
    backs.extend(((end - 1, 2), (1, 2)))
    first = segments - 2 * QUAD
    for octet in range(1, octets - 1):
        (leaving,) = call(octet_exit_body, [wide], low, high, quad, far)
        source = 2 * octet
        if octet == octets - 2:
            pairs = [(i, i + 2 * QUAD) for i in range(first - 2 * QUAD, first)]
            late = quads_swapped(quad, [(end, end + 1)])
            low = lax.ppermute(leaving, AXES, pairs)
        else:
            pairs = [(source, source + 2), (source + 1, source + 3)]
            low = high = quads_swapped(leaving, pairs)
            backs.append((source + 1, len(rows)))
        entries.append((source + 2, len(rows)))
        entries.append((source + 3, len(rows)))
        rows.append(low)
    (prefix,) = call(
        prefix_body, [shape], *parts, far, late, leaving, scratch=[held]
    )
    return call(
        functools.partial(last_body, entries, backs, len(rows)),
        [line, line], *rows, final, beside, far, late, prefix,
    )


def solution(mesh):
    return jax.shard_map(
        on_device,
        mesh=mesh,
        in_specs=(
            P(("grp", "seg"), None),
            P(("grp", "seg"), None, None),
            P(),
            P("grp", None),
            P(("grp", "seg"), None),
        ),
        out_specs=(P(("grp", "seg"), None), P(("grp", "seg"), None)),
        check_vma=False,
    )
```

```python
import functools
import jax
import jax.numpy as jnp
from jax import lax
from jax.experimental import pallas as pl
from jax.experimental.pallas import tpu as pltpu
from jax.sharding import PartitionSpec as P


AXES = ("grp", "seg")
PAD = 8
QUAD = 4
VMEM = pl.BlockSpec(memory_space=pltpu.VMEM)
HBM = pl.BlockSpec(memory_space=pltpu.HBM)
F32 = jnp.float32


def halves(a):
    high = a.astype(jnp.bfloat16)
    return high, (a - high.astype(jnp.float32)).astype(jnp.bfloat16)


def dot(a, b, dims=((1,), (0,))):
    def one(x, y):
        return lax.dot_general(
            x, y, (dims, ((), ())), preferred_element_type=jnp.float32
        )

    (ah, al), (bh, bl) = halves(a), halves(b)
    return one(ah, bh) + (one(ah, bl) + one(al, bh))


def times(row, mat):
    n = mat.shape[0]
    on = lax.broadcasted_iota(jnp.int32, (n, n), 0) == lax.broadcasted_iota(
        jnp.int32, (n, n), 1
    )
    column = jnp.sum(jnp.where(on, row, 0.0), axis=1, keepdims=True)
    return jnp.sum(mat * column, axis=0, keepdims=True)


def call(body, shapes, *args, scratch=(), raw=False):
    out = tuple(jax.ShapeDtypeStruct(*s) for s in shapes)
    return pl.pallas_call(
        body,
        out_shape=out,
        in_specs=[HBM if raw else VMEM] * len(args),
        out_specs=tuple(VMEM for _ in out),
        scratch_shapes=list(scratch),
        compiler_params=pltpu.CompilerParams(vmem_limit_bytes=8 << 20),
    )(*args)


def where_am_i():
    return lax.axis_index("grp") * lax.axis_size("seg") + lax.axis_index("seg")


def put_composed(ref, earlier, later):
    width = later.shape[1]
    both = dot(earlier, later[:width])
    ref[:width] = both[:width]
    ref[width:] = both[width:] + later[width:]


def lookup(table, index, base):
    rows, width = table.shape
    level = lax.broadcasted_iota(jnp.int32, (rows, width), 0) + base
    kept = table[...]
    found = [
        jnp.sum(jnp.where(index[k : k + 1, :] == level, kept, 0.0), axis=0, keepdims=True)
        for k in range(index.shape[0])
    ]
    return jnp.concatenate(found, axis=0)


def early_body(
    inv_len, nodes_in, loss_in, jac_in, own_in, index_in,
    nodes, loss, jac, index, near, sens, state, own, sems,
):
    steps, width, _ = jac.shape
    pairs = [(index_in, index), (own_in, own), (nodes_in, nodes), (loss_in, loss)]
    pairs += [(jac_in.at[k], jac.at[k]) for k in range(steps)]
    copies = [
        pltpu.make_async_copy(src, dst, sems.at[k]) for k, (src, dst) in enumerate(pairs)
    ]
    for copy in copies:
        copy.start()
    for copy in copies[:4]:
        copy.wait()
    near[...] = lookup(own, index, lax.axis_index("grp") * own.shape[0])
    start = jnp.broadcast_to(nodes[...], (PAD, width))
    rates = loss[...]
    slope = jnp.tanh(start)
    weight = inv_len * (rates * (1.0 - slope * slope))
    row = lax.broadcasted_iota(jnp.int32, (width, width), 0)
    col = lax.broadcasted_iota(jnp.int32, (width, width), 1)
    first = jnp.where(row == col, weight[:1], 0.0)
    copies[4].wait()
    both = dot(
        jnp.concatenate([first, -inv_len * rates * slope], axis=0), jac[0], ((1,), (1,))
    )
    sens[...] = jnp.where(row == col, 1.0, 0.0) - both[:width]
    state[...] = start + both[width:]
    for copy in copies[5:]:
        copy.wait()


def local_body(
    inv_len, src_scale, other, nodes, loss, jac, index, near, sens_in, state_in,
    top, bottom, final,
):
    steps, width, _ = jac.shape
    cut = top.shape[0]
    rows = other.shape[0]
    source = near[...] + lookup(other, index, (1 - lax.axis_index("grp")) * rows)
    rates = loss[...]
    sens = sens_in[...]
    spread = jnp.sum(jac[0] * (src_scale * source[:1]), axis=1, keepdims=True)
    on = lax.broadcasted_iota(jnp.int32, (width, width), 0) == lax.broadcasted_iota(
        jnp.int32, (width, width), 1
    )
    state = state_in[...] + jnp.sum(jnp.where(on, spread, 0.0), axis=0, keepdims=True)
    for step in range(1, steps):
        slope = jnp.tanh(state)
        weight = inv_len * (rates * (1.0 - slope * slope))
        drive = src_scale * source[step : step + 1] - inv_len * rates * slope
        both = dot(
            jnp.concatenate([sens * weight[:1], drive], axis=0), jac[step], ((1,), (1,))
        )
        sens = sens - both[:width]
        state = state + both[width:]
    sens = jnp.where(where_am_i() == 0, 0.0, sens)
    top[...] = sens[:cut]
    bottom[: width - cut] = sens[cut:]
    offset = state - jnp.broadcast_to(times(nodes[...], sens), state.shape)
    bottom[width - cut :] = offset
    bottom[width - cut + 1 : width - cut + 2] = nodes[...]
    final[...] = state[:1]


def in_order(held, parts):
    member = lax.rem(where_am_i(), QUAD)
    cut = parts[0].shape[0]
    for k in range(QUAD):
        by = jnp.where(lax.axis_index("grp") == 0, k, 3 - k) if k in (1, 2) else k
        place = jnp.bitwise_xor(member, by)
        held[place, :cut] = parts[2 * k][...]
        held[place, cut:] = parts[2 * k + 1][...]


def follow(entry, mapping):
    width = mapping.shape[1]
    return times(entry, mapping[:width]) + mapping[width : width + 1]


def first_exit_body(*refs):
    *parts, leaving = refs
    place = where_am_i()
    width = leaving.shape[1]
    cut = parts[0].shape[0]

    def step(state, k):
        upper, lower = parts[2 * k : 2 * k + 2]
        rest = width - cut
        n = lax.broadcasted_iota(jnp.int32, (width, width), 0)
        on = n == lax.broadcasted_iota(jnp.int32, (width, width), 1)
        column = jnp.sum(jnp.where(on, state, 0.0), axis=1, keepdims=True)
        return (
            jnp.sum(upper[...] * column[:cut], axis=0, keepdims=True)
            + jnp.sum(lower[:rest] * column[cut:], axis=0, keepdims=True)
            + lower[rest : rest + 1]
        )

    leaving[...] = jnp.zeros_like(leaving)
    for member in range(QUAD):

        @pl.when(lax.rem(place, QUAD) == member)
        def _():
            node = width - cut + 1
            leaving[1:2] = parts[2 * member + 1][node : node + 1]

        @pl.when(place == member)
        def _():
            state = parts[2 * member + 1][width - cut : width - cut + 1]
            for k in range(1, QUAD):
                state = step(state, member ^ k)
            leaving[:1] = state


def join(ref, k, top, bottom):
    cut = top.shape[0]
    ref[k, :cut] = top[...]
    ref[k, cut:] = bottom[...]


def pair_body(top, bottom, top1, bottom1, top2, bottom2, total, held):
    width = total.shape[1]
    node = slice(width + 1, width + 2)
    side = lax.rem(where_am_i(), 2)
    join(held, side, top, bottom)
    straight = lax.axis_index("grp") == 0

    @pl.when(straight)
    def _():
        join(held, 1 - side, top1, bottom1)

    @pl.when(jnp.logical_not(straight))
    def _():
        join(held, 1 - side, top2, bottom2)

    put_composed(total, held[0], held[1])
    total[node] = held[0, node]


def quad_body(
    pair, top1, bottom1, top2, bottom2, top3, bottom3, total, beside, held
):
    width = total.shape[1]
    node = slice(width + 1, width + 2)
    side = lax.rem(where_am_i(), 2)
    upper = lax.rem(lax.div(where_am_i(), 2), 2) == 1
    straight = lax.axis_index("grp") == 0

    @pl.when(straight)
    def _():
        join(held, side, top2, bottom2)

    @pl.when(jnp.logical_not(straight))
    def _():
        join(held, side, top1, bottom1)

    join(held, 1 - side, top3, bottom3)
    end = bottom1.shape[0] - PAD + 1
    one, two = bottom1[end : end + 1], bottom2[end : end + 1]
    near, far = jnp.where(straight, one, two), bottom3[end : end + 1]
    beside[...] = jnp.where(side == 0, near, far)

    @pl.when(where_am_i() < QUAD)
    def _():
        total[...] = jnp.zeros_like(total)

    @pl.when(where_am_i() >= QUAD)
    def _():
        head = jnp.where(upper, held[0, node], pair[node])
        put_composed(held.at[2], held[0], held[1])

        @pl.when(upper)
        def _():
            put_composed(total, held[2], pair[...])

        @pl.when(jnp.logical_not(upper))
        def _():
            put_composed(total, pair[...], held[2])

        total[node] = head


def is_upper():
    return lax.rem(lax.div(where_am_i(), QUAD), 2) == 1


def is_last():
    count = lax.axis_size("grp") * lax.axis_size("seg")
    return where_am_i() >= count - 2 * QUAD


def prefix_body(*refs):
    *parts, far, late, after, prefix, held = refs
    in_order(held, parts)
    member = lax.rem(where_am_i(), QUAD)
    prefix[...] = held[0]

    @pl.when(is_upper() & jnp.logical_not(is_last()) & (where_am_i() >= 2 * QUAD))
    def _():
        put_composed(prefix, far[...], held[0])

    @pl.when(is_upper() & is_last())
    def _():
        put_composed(prefix, late[...], held[0])

    for k in range(1, QUAD):

        @pl.when(member >= k)
        def _():
            put_composed(prefix, prefix[...], held[k])


def quad_exit_body(entry, mapping, out):
    width = mapping.shape[1]
    out[...] = jnp.zeros_like(out)
    out[:1] = follow(entry[:1], mapping[...])
    out[1:2] = mapping[width + 1 : width + 2]


def octet_exit_body(low, high, own, far, out):
    upper = is_upper()
    width = own.shape[1]
    out[...] = jnp.zeros_like(out)

    @pl.when(upper)
    def _():
        out[:1] = follow(follow(high[:1], far[...]), own[...])
        out[1:2] = far[width + 1 : width + 2]

    @pl.when(jnp.logical_not(upper))
    def _():
        out[:1] = follow(follow(low[:1], own[...]), far[...])
        out[1:2] = own[width + 1 : width + 2]


def last_body(entries, backs, count, *refs):
    rows = refs[:count]
    final, beside, far, late, mapping, out, defect = refs[count:]
    place = where_am_i()
    width = out.shape[1]
    end = lax.rem(place, QUAD) == QUAD - 1
    quad = lax.div(place, QUAD)
    entry = jnp.zeros_like(out)
    for target, k in entries:
        entry = jnp.where(quad == target, rows[k][:1], entry)
    node = slice(width + 1, width + 2)
    following = jnp.where(is_last(), late[node], far[node])
    following = jnp.where(is_upper(), 0.0, following)
    for target, k in backs:
        following = jnp.where(quad == target, rows[k][1:2], following)
    following = jnp.where(end, following, beside[...])
    out[...] = follow(entry, mapping[...])
    defect[...] = final[...] - following


def on_device(nodes, jac_inverse, loss_rates, rate_table, rate_index):
    steps, width, _ = jac_inverse.shape
    seg_count = lax.axis_size("seg")
    segments = lax.axis_size("grp") * seg_count
    inv_len = 1.0 / (steps * segments)
    src_scale = 0.25 / steps

    def swapped(array, by):
        return lax.ppermute(array, AXES, [(i, i ^ by) for i in range(segments)])

    other = swapped(rate_table, seg_count)
    shape = ((width + PAD, width), F32)
    line = ((1, width), F32)
    early = call(
        functools.partial(early_body, inv_len),
        [
            line, line, (jac_inverse.shape, F32), (rate_index.shape, jnp.int32),
            ((steps, width), F32), ((width, width), F32), ((PAD, width), F32),
        ],
        *(
            pltpu.with_memory_space_constraint(array, pltpu.HBM)
            for array in (nodes, loss_rates[None], jac_inverse, rate_table, rate_index)
        ),
        scratch=[pltpu.VMEM(rate_table.shape, F32), pltpu.SemaphoreType.DMA((4 + steps,))],
        raw=True,
    )
    cut = width // 2
    halves = [((cut, width), F32), ((width - cut + PAD, width), F32)]
    top, bottom, final = call(
        functools.partial(local_body, inv_len, src_scale),
        [*halves, line], other, *early,
    )

    def turned(array, by):
        pairs = [(i, i ^ (by if i < seg_count else 3 - by)) for i in range(segments)]
        return lax.ppermute(array, AXES, pairs)

    top1 = turned(top, 1)
    bottom2 = turned(bottom, 2)
    bottom1 = turned(bottom, 1)
    top2 = turned(top, 2)
    top3 = turned(top1, 2)
    bottom3 = turned(bottom2, 1)
    parts = [top, bottom, top1, bottom1, top2, bottom2, top3, bottom3]
    wide = ((2, width), F32)
    held = pltpu.VMEM((QUAD, *shape[0]), F32)
    octets = segments // (2 * QUAD)

    def quads_swapped(array, quad_pairs):
        to = {}
        for one, two in quad_pairs:
            for k in range(QUAD):
                to[one * QUAD + k] = two * QUAD + k
                to[two * QUAD + k] = one * QUAD + k
        busy = set(to)
        for i in range(segments):
            if i not in busy:
                core = (i + seg_count) % segments
                to[i] = i ^ 1 if core in busy else core
        return lax.ppermute(array, AXES, sorted(to.items()))

    (leaving,) = call(first_exit_body, [wide], *parts)
    rows, entries, backs = [], [], []

    row = quads_swapped(leaving, [(0, 1)])
    rows.append(row)
    entries.append((1, 0))
    backs.append((0, 0))
    (pair,) = call(pair_body, [shape], *parts[:6], scratch=[held])
    quad, beside = call(
        quad_body, [shape, line], pair, *parts[2:], scratch=[held]
    )
    far = quads_swapped(quad, [(2 * o, 2 * o + 1) for o in range(1, octets - 1)])

    (leaving,) = call(quad_exit_body, [wide], row, quad)
    end = 2 * octets - 2
    high = quads_swapped(leaving, [(1, 3)])
    low = quads_swapped(leaving, [(1, 2), (end - 1, end)])
    rows.extend((high, low))
    entries.extend(((3, 1), (2, 2)))
    backs.extend(((end - 1, 2), (1, 2)))
    first = segments - 2 * QUAD
    for octet in range(1, octets - 1):
        (leaving,) = call(octet_exit_body, [wide], low, high, quad, far)
        source = 2 * octet
        if octet == octets - 2:
            pairs = [(i, i + 2 * QUAD) for i in range(first - 2 * QUAD, first)]
            late = quads_swapped(quad, [(end, end + 1)])
            low = lax.ppermute(leaving, AXES, pairs)
        else:
            pairs = [(source, source + 2), (source + 1, source + 3)]
            low = high = quads_swapped(leaving, pairs)
            backs.append((source + 1, len(rows)))
        entries.append((source + 2, len(rows)))
        entries.append((source + 3, len(rows)))
        rows.append(low)
    (prefix,) = call(
        prefix_body, [shape], *parts, far, late, leaving, scratch=[held]
    )
    return call(
        functools.partial(last_body, entries, backs, len(rows)),
        [line, line], *rows, final, beside, far, late, prefix,
    )


def solution(mesh):
    return jax.shard_map(
        on_device,
        mesh=mesh,
        in_specs=(
            P(("grp", "seg"), None),
            P(("grp", "seg"), None, None),
            P(),
            P("grp", None),
            P(("grp", "seg"), None),
        ),
        out_specs=(P(("grp", "seg"), None), P(("grp", "seg"), None)),
        check_vma=False,
    )
```

```python
import functools
import jax
import jax.numpy as jnp
from jax import lax
from jax.experimental import pallas as pl
from jax.experimental.pallas import tpu as pltpu
from jax.sharding import PartitionSpec as P


AXES = ("grp", "seg")
PAD = 8
QUAD = 4
VMEM = pl.BlockSpec(memory_space=pltpu.VMEM)
HBM = pl.BlockSpec(memory_space=pltpu.HBM)
F32 = jnp.float32


def halves(a):
    high = a.astype(jnp.bfloat16)
    return high, (a - high.astype(jnp.float32)).astype(jnp.bfloat16)


def dot(a, b, dims=((1,), (0,))):
    def one(x, y):
        return lax.dot_general(
            x, y, (dims, ((), ())), preferred_element_type=jnp.float32
        )

    (ah, al), (bh, bl) = halves(a), halves(b)
    return one(ah, bh) + (one(ah, bl) + one(al, bh))


def times(row, mat):
    n = mat.shape[0]
    on = lax.broadcasted_iota(jnp.int32, (n, n), 0) == lax.broadcasted_iota(
        jnp.int32, (n, n), 1
    )
    column = jnp.sum(jnp.where(on, row, 0.0), axis=1, keepdims=True)
    return jnp.sum(mat * column, axis=0, keepdims=True)


def call(body, shapes, *args, scratch=(), raw=False):
    out = tuple(jax.ShapeDtypeStruct(*s) for s in shapes)
    return pl.pallas_call(
        body,
        out_shape=out,
        in_specs=[HBM if raw else VMEM] * len(args),
        out_specs=tuple(VMEM for _ in out),
        scratch_shapes=list(scratch),
        compiler_params=pltpu.CompilerParams(vmem_limit_bytes=8 << 20),
    )(*args)


def where_am_i():
    return lax.axis_index("grp") * lax.axis_size("seg") + lax.axis_index("seg")


def put_composed(ref, earlier, later):
    width = later.shape[1]
    both = dot(earlier, later[:width])
    ref[:width] = both[:width]
    ref[width:] = both[width:] + later[width:]


def lookup(table, index, base):
    rows, width = table.shape
    level = lax.broadcasted_iota(jnp.int32, (rows, width), 0) + base
    kept = table[...]
    found = [
        jnp.sum(jnp.where(index[k : k + 1, :] == level, kept, 0.0), axis=0, keepdims=True)
        for k in range(index.shape[0])
    ]
    return jnp.concatenate(found, axis=0)


def early_body(
    inv_len, nodes_in, loss_in, jac_in, own_in, index_in,
    nodes, loss, jac, index, near, sens, state, own, sems,
):
    steps, width, _ = jac.shape
    pairs = [(index_in, index), (own_in, own), (nodes_in, nodes), (loss_in, loss)]
    pairs += [(jac_in.at[k], jac.at[k]) for k in range(steps)]
    copies = [
        pltpu.make_async_copy(src, dst, sems.at[k]) for k, (src, dst) in enumerate(pairs)
    ]
    for copy in copies:
        copy.start()
    for copy in copies[:4]:
        copy.wait()
    near[...] = lookup(own, index, lax.axis_index("grp") * own.shape[0])
    start = jnp.broadcast_to(nodes[...], (PAD, width))
    rates = loss[...]
    slope = jnp.tanh(start)
    weight = inv_len * (rates * (1.0 - slope * slope))
    row = lax.broadcasted_iota(jnp.int32, (width, width), 0)
    col = lax.broadcasted_iota(jnp.int32, (width, width), 1)
    first = jnp.where(row == col, weight[:1], 0.0)
    copies[4].wait()
    both = dot(
        jnp.concatenate([first, -inv_len * rates * slope], axis=0), jac[0], ((1,), (1,))
    )
    sens[...] = jnp.where(row == col, 1.0, 0.0) - both[:width]
    state[...] = start + both[width:]
    for copy in copies[5:]:
        copy.wait()


def local_body(
    inv_len, src_scale, other, nodes, loss, jac, index, near, sens_in, state_in,
    top, bottom, final,
):
    steps, width, _ = jac.shape
    cut = top.shape[0]
    rows = other.shape[0]
    source = near[...] + lookup(other, index, (1 - lax.axis_index("grp")) * rows)
    rates = loss[...]
    sens = sens_in[...]
    spread = jnp.sum(jac[0] * (src_scale * source[:1]), axis=1, keepdims=True)
    on = lax.broadcasted_iota(jnp.int32, (width, width), 0) == lax.broadcasted_iota(
        jnp.int32, (width, width), 1
    )
    state = state_in[...] + jnp.sum(jnp.where(on, spread, 0.0), axis=0, keepdims=True)
    for step in range(1, steps):
        slope = jnp.tanh(state)
        weight = inv_len * (rates * (1.0 - slope * slope))
        drive = src_scale * source[step : step + 1] - inv_len * rates * slope
        both = dot(
            jnp.concatenate([sens * weight[:1], drive], axis=0), jac[step], ((1,), (1,))
        )
        sens = sens - both[:width]
        state = state + both[width:]
    sens = jnp.where(where_am_i() == 0, 0.0, sens)
    top[...] = sens[:cut]
    bottom[: width - cut] = sens[cut:]
    offset = state - jnp.broadcast_to(times(nodes[...], sens), state.shape)
    bottom[width - cut :] = offset
    bottom[width - cut + 1 : width - cut + 2] = nodes[...]
    final[...] = state[:1]


def in_order(held, parts):
    member = lax.rem(where_am_i(), QUAD)
    cut = parts[0].shape[0]
    for k in range(QUAD):
        by = jnp.where(lax.axis_index("grp") == 0, k, 3 - k) if k in (1, 2) else k
        place = jnp.bitwise_xor(member, by)
        held[place, :cut] = parts[2 * k][...]
        held[place, cut:] = parts[2 * k + 1][...]


def follow(entry, mapping):
    width = mapping.shape[1]
    return times(entry, mapping[:width]) + mapping[width : width + 1]


def first_exit_body(*refs):
    *parts, leaving = refs
    place = where_am_i()
    width = leaving.shape[1]
    cut = parts[0].shape[0]

    def step(state, k):
        upper, lower = parts[2 * k : 2 * k + 2]
        rest = width - cut
        n = lax.broadcasted_iota(jnp.int32, (width, width), 0)
        on = n == lax.broadcasted_iota(jnp.int32, (width, width), 1)
        column = jnp.sum(jnp.where(on, state, 0.0), axis=1, keepdims=True)
        return (
            jnp.sum(upper[...] * column[:cut], axis=0, keepdims=True)
            + jnp.sum(lower[:rest] * column[cut:], axis=0, keepdims=True)
            + lower[rest : rest + 1]
        )

    leaving[...] = jnp.zeros_like(leaving)
    for member in range(QUAD):

        @pl.when(lax.rem(place, QUAD) == member)
        def _():
            node = width - cut + 1
            leaving[1:2] = parts[2 * member + 1][node : node + 1]

        @pl.when(place == member)
        def _():
            state = parts[2 * member + 1][width - cut : width - cut + 1]
            for k in range(1, QUAD):
                state = step(state, member ^ k)
            leaving[:1] = state


def join(ref, k, top, bottom):
    cut = top.shape[0]
    ref[k, :cut] = top[...]
    ref[k, cut:] = bottom[...]


def pair_body(top, bottom, top1, bottom1, top2, bottom2, total, held):
    width = total.shape[1]
    node = slice(width + 1, width + 2)
    side = lax.rem(where_am_i(), 2)
    join(held, side, top, bottom)
    straight = lax.axis_index("grp") == 0

    @pl.when(straight)
    def _():
        join(held, 1 - side, top1, bottom1)

    @pl.when(jnp.logical_not(straight))
    def _():
        join(held, 1 - side, top2, bottom2)

    put_composed(total, held[0], held[1])
    total[node] = held[0, node]


def quad_body(
    pair, top1, bottom1, top2, bottom2, top3, bottom3, total, beside, held
):
    width = total.shape[1]
    node = slice(width + 1, width + 2)
    side = lax.rem(where_am_i(), 2)
    upper = lax.rem(lax.div(where_am_i(), 2), 2) == 1
    straight = lax.axis_index("grp") == 0

    @pl.when(straight)
    def _():
        join(held, side, top2, bottom2)

    @pl.when(jnp.logical_not(straight))
    def _():
        join(held, side, top1, bottom1)

    join(held, 1 - side, top3, bottom3)
    end = bottom1.shape[0] - PAD + 1
    one, two = bottom1[end : end + 1], bottom2[end : end + 1]
    near, far = jnp.where(straight, one, two), bottom3[end : end + 1]
    beside[...] = jnp.where(side == 0, near, far)

    @pl.when(where_am_i() < QUAD)
    def _():
        total[...] = jnp.zeros_like(total)

    @pl.when(where_am_i() >= QUAD)
    def _():
        head = jnp.where(upper, held[0, node], pair[node])
        put_composed(held.at[2], held[0], held[1])

        @pl.when(upper)
        def _():
            put_composed(total, held[2], pair[...])

        @pl.when(jnp.logical_not(upper))
        def _():
            put_composed(total, pair[...], held[2])

        total[node] = head


def is_upper():
    return lax.rem(lax.div(where_am_i(), QUAD), 2) == 1


def is_last():
    count = lax.axis_size("grp") * lax.axis_size("seg")
    return where_am_i() >= count - 2 * QUAD


def prefix_body(*refs):
    *parts, far, late, after, prefix, held = refs
    in_order(held, parts)
    member = lax.rem(where_am_i(), QUAD)
    prefix[...] = held[0]

    @pl.when(is_upper() & jnp.logical_not(is_last()) & (where_am_i() >= 2 * QUAD))
    def _():
        put_composed(prefix, far[...], held[0])

    @pl.when(is_upper() & is_last())
    def _():
        put_composed(prefix, late[...], held[0])

    for k in range(1, QUAD):

        @pl.when(member >= k)
        def _():
            put_composed(prefix, prefix[...], held[k])


def quad_exit_body(entry, mapping, out):
    width = mapping.shape[1]
    out[...] = jnp.zeros_like(out)
    out[1:2] = mapping[width + 1 : width + 2]

    @pl.when(lax.div(where_am_i(), QUAD) == 1)
    def _():
        out[:1] = follow(entry[:1], mapping[...])


def octet_exit_body(octet, low, high, own, far, out):
    upper = is_upper()
    inside = lax.div(where_am_i(), 2 * QUAD) == octet
    node = slice(own.shape[1] + 1, own.shape[1] + 2)
    out[...] = jnp.zeros_like(out)
    out[1:2] = jnp.where(upper, far[node], own[node])

    @pl.when(inside & upper)
    def _():
        out[:1] = follow(follow(high[:1], far[...]), own[...])

    @pl.when(inside & jnp.logical_not(upper))
    def _():
        out[:1] = follow(follow(low[:1], own[...]), far[...])


def last_body(entries, backs, count, *refs):
    rows = refs[:count]
    final, beside, far, late, mapping, out, defect = refs[count:]
    place = where_am_i()
    width = out.shape[1]
    end = lax.rem(place, QUAD) == QUAD - 1
    quad = lax.div(place, QUAD)
    entry = jnp.zeros_like(out)
    for target, k in entries:
        entry = jnp.where(quad == target, rows[k][:1], entry)
    node = slice(width + 1, width + 2)
    following = jnp.where(is_last(), late[node], far[node])
    following = jnp.where(is_upper(), 0.0, following)
    for target, k in backs:
        following = jnp.where(quad == target, rows[k][1:2], following)
    following = jnp.where(end, following, beside[...])
    out[...] = follow(entry, mapping[...])
    defect[...] = final[...] - following


def on_device(nodes, jac_inverse, loss_rates, rate_table, rate_index):
    steps, width, _ = jac_inverse.shape
    seg_count = lax.axis_size("seg")
    segments = lax.axis_size("grp") * seg_count
    inv_len = 1.0 / (steps * segments)
    src_scale = 0.25 / steps

    def swapped(array, by):
        return lax.ppermute(array, AXES, [(i, i ^ by) for i in range(segments)])

    other = swapped(rate_table, seg_count)
    shape = ((width + PAD, width), F32)
    line = ((1, width), F32)
    early = call(
        functools.partial(early_body, inv_len),
        [
            line, line, (jac_inverse.shape, F32), (rate_index.shape, jnp.int32),
            ((steps, width), F32), ((width, width), F32), ((PAD, width), F32),
        ],
        *(
            pltpu.with_memory_space_constraint(array, pltpu.HBM)
            for array in (nodes, loss_rates[None], jac_inverse, rate_table, rate_index)
        ),
        scratch=[pltpu.VMEM(rate_table.shape, F32), pltpu.SemaphoreType.DMA((4 + steps,))],
        raw=True,
    )
    cut = width // 2
    halves = [((cut, width), F32), ((width - cut + PAD, width), F32)]
    top, bottom, final = call(
        functools.partial(local_body, inv_len, src_scale),
        [*halves, line], other, *early,
    )

    def turned(array, by):
        pairs = [(i, i ^ (by if i < seg_count else 3 - by)) for i in range(segments)]
        return lax.ppermute(array, AXES, pairs)

    top1 = turned(top, 1)
    bottom2 = turned(bottom, 2)
    bottom1 = turned(bottom, 1)
    top2 = turned(top, 2)
    top3 = turned(top1, 2)
    bottom3 = turned(bottom2, 1)
    parts = [top, bottom, top1, bottom1, top2, bottom2, top3, bottom3]
    wide = ((2, width), F32)
    held = pltpu.VMEM((QUAD, *shape[0]), F32)
    octets = segments // (2 * QUAD)

    def quads_swapped(array, quad_pairs):
        to = {}
        for one, two in quad_pairs:
            for k in range(QUAD):
                to[one * QUAD + k] = two * QUAD + k
                to[two * QUAD + k] = one * QUAD + k
        busy = set(to)
        for i in range(segments):
            if i not in busy:
                core = (i + seg_count) % segments
                to[i] = i ^ 1 if core in busy else core
        return lax.ppermute(array, AXES, sorted(to.items()))

    (leaving,) = call(first_exit_body, [wide], *parts)
    rows, entries, backs = [], [], []

    row = quads_swapped(leaving, [(0, 1)])
    rows.append(row)
    entries.append((1, 0))
    backs.append((0, 0))
    (pair,) = call(pair_body, [shape], *parts[:6], scratch=[held])
    quad, beside = call(
        quad_body, [shape, line], pair, *parts[2:], scratch=[held]
    )
    far = quads_swapped(quad, [(2 * o, 2 * o + 1) for o in range(1, octets - 1)])

    (leaving,) = call(quad_exit_body, [wide], row, quad)
    end = 2 * octets - 2
    high = quads_swapped(leaving, [(1, 3)])
    low = quads_swapped(leaving, [(1, 2), (end - 1, end)])
    rows.extend((high, low))
    entries.extend(((3, 1), (2, 2)))
    backs.extend(((end - 1, 2), (1, 2)))
    first = segments - 2 * QUAD
    for octet in range(1, octets - 1):
        body = functools.partial(octet_exit_body, octet)
        (leaving,) = call(body, [wide], low, high, quad, far)
        source = 2 * octet
        if octet == octets - 2:
            pairs = [(i, i + 2 * QUAD) for i in range(first - 2 * QUAD, first)]
            late = quads_swapped(quad, [(end, end + 1)])
            low = lax.ppermute(leaving, AXES, pairs)
        else:
            pairs = [(source, source + 2), (source + 1, source + 3)]
            low = high = quads_swapped(leaving, pairs)
            backs.append((source + 1, len(rows)))
        entries.append((source + 2, len(rows)))
        entries.append((source + 3, len(rows)))
        rows.append(low)
    (prefix,) = call(
        prefix_body, [shape], *parts, far, late, leaving, scratch=[held]
    )
    return call(
        functools.partial(last_body, entries, backs, len(rows)),
        [line, line], *rows, final, beside, far, late, prefix,
    )


def solution(mesh):
    return jax.shard_map(
        on_device,
        mesh=mesh,
        in_specs=(
            P(("grp", "seg"), None),
            P(("grp", "seg"), None, None),
            P(),
            P("grp", None),
            P(("grp", "seg"), None),
        ),
        out_specs=(P(("grp", "seg"), None), P(("grp", "seg"), None)),
        check_vma=False,
    )
```
